512 devices in a mesh: row: 32 (over y_hi, z), proto: 16 (over x, y_lo, core).
Axes of the slice: x: 4, y: 8 (y_hi: 4, y_lo: 2; y = y_hi * 2 + y_lo), z: 8, core: 2. Of those that a mesh axis runs over, the one named last changes fastest.
Arguments:
- embeddings: bfloat16 [8192, 128], P('row'), may hold values from -6.75 to 6.75
- second_view: bfloat16 [8192, 128], P('row'), may hold values from -6.75 to 6.75
- prototypes: bfloat16 [65536, 128], P('proto'), may hold values from -6.75 to 6.75
- row_scale: float32 [8192], P('row'), may hold values from 1 to 16, as said below
- col_scale: float32 [65536], P('proto'), may hold values from 1 to 16, as said below
Outputs:
- embed_grad: float32 [8192, 128], P(('row', 'proto'))
- proto_grad: float32 [65536, 128], P(('proto', 'row'))
The draws below stay inside these ranges and needn't reach their ends.
Inputs may be any that keep to these rules, and one draw needn't show every extreme that they name: `row_scale`: positive scalings. `col_scale`: positive scalings.
All inputs are finite; a program needn't handle non-finite values.
Results may differ from the reference program's by a relative error of at most 0.0025.
Values may be sent and summed in bfloat16 or wider, within the bound.
A program may use at most 64 MiB of HBM per device.

```python
import math
import jax
import jax.numpy as jnp
from jax import lax

D = 128
ROWS_DEV = 256
ITERS = 4
ROWS = 8192
PROTOS = 65536
N_ROW = 32


def spread_draw(key, row_total):
    noise_key, sign_key, size_key = jax.random.split(key, 3)
    values = jax.random.normal(noise_key, (row_total, D), jnp.float32)
    lead_size = jnp.array([3.7, 2.5], jnp.float32)
    values = jnp.clip(values, -3.0, 3.0)
    signs = jnp.where(jax.random.bernoulli(sign_key, 0.5, (row_total, 2)), 1.0, -1.0)
    factors = jax.random.uniform(size_key, (row_total, 2), jnp.float32, minval=0.7, maxval=1.3)
    leading = signs * factors * lead_size[None, :]
    return jnp.concatenate((leading, values[:, 2:]), 1)


def view_draw(key, row_total):
    first = spread_draw(jax.random.fold_in(key, 7), row_total)
    noise_key, mean_key, rest_key = jax.random.split(jax.random.fold_in(key, 13), 3)
    noise = jnp.clip(jax.random.normal(noise_key, (row_total, D), jnp.float32), -3.0, 3.0)
    lead_mean = 3.5
    mean_signs = jnp.where(jax.random.bernoulli(mean_key, 0.5, (2,)), 1.0, -1.0)
    common = jnp.concatenate((lead_mean * mean_signs, 0.3 * jax.random.normal(rest_key, (D - 2,), jnp.float32)))
    lead_mask = jnp.arange(D) < 2
    first_mix = jnp.where(lead_mask, 0.4, 0.6)
    noise_mix = jnp.where(lead_mask, 0.5, 0.8)
    values = common[None, :] + first_mix[None, :] * first + noise_mix[None, :] * noise
    return jnp.clip(values, -6.75, 6.75)


def scale_draw(key, length):
    position = jnp.arange(length).astype(jnp.float32) / length
    jitter = jax.random.uniform(key, (length,), jnp.float32, minval=-0.3, maxval=2.9)
    logs = jnp.clip(math.log(3.0) * position + jitter, 0.0, math.log(16.0))
    return jnp.clip(jnp.exp(logs), 1.0, 16.0)


def draw_embeddings(key, part):
    return spread_draw(jax.random.fold_in(key, 7), ROWS).astype(jnp.bfloat16)


def draw_second_view(key, part):
    return view_draw(key, ROWS).astype(jnp.bfloat16)


def draw_prototypes(key, part):
    return spread_draw(jax.random.fold_in(key, 11), PROTOS).astype(jnp.bfloat16)


def draw_row_scale(key, part):
    return scale_draw(jax.random.fold_in(key, 3), ROWS)


def draw_col_scale(key, part):
    return scale_draw(jax.random.fold_in(key, 5), PROTOS)


def setup_inputs(seed: int = 0) -> dict:
    key_list = jax.random.split(jax.random.key(seed), 6)
    embeddings = draw_embeddings(jax.random.fold_in(key_list[5], 71), 0)
    second_view = draw_second_view(jax.random.fold_in(key_list[5], 71), 0)
    prototypes = draw_prototypes(jax.random.fold_in(key_list[5], 71), 0)
    row_scale = draw_row_scale(jax.random.fold_in(key_list[5], 71), 0)
    col_scale = draw_col_scale(jax.random.fold_in(key_list[5], 71), 0)
    return {"embeddings": embeddings, "second_view": second_view, "prototypes": prototypes, "row_scale": row_scale, "col_scale": col_scale}


def reference(embeddings, second_view, prototypes, row_scale, col_scale):
    logit_scale = 1.0 / (0.05 * D)
    view_scale = 1.0 / (0.1 * D)
    plan_mass = 64.0 * PROTOS
    proto_wide = prototypes.astype(jnp.float32)
    emb_blocks = embeddings.reshape(N_ROW, ROWS_DEV, D)
    view_blocks = second_view.reshape(N_ROW, ROWS_DEV, D)
    scale_blocks = row_scale.reshape(N_ROW, ROWS_DEV)

    def plan_block(emb_block, scale_block):
        logits = jnp.dot(emb_block.astype(jnp.float32), proto_wide.T) * logit_scale
        return scale_block[:, None] * col_scale[None, :] * jnp.exp(logits) / plan_mass

    def cot_block(view_block):
        return -jnp.dot(view_block.astype(jnp.float32), proto_wide.T) * view_scale

    zero_cols = jnp.zeros((PROTOS,), jnp.float32)

    def first_pass(running, blocks):
        emb_block, view_block, scale_block = blocks
        plan = plan_block(emb_block, scale_block)
        weighted = plan * cot_block(view_block)
        return (running[0] + plan.sum(0), running[1] + weighted.sum(0)), (plan.sum(1), weighted.sum(1))

    (col_mass, col_weight), (row_mass, row_weight) = lax.scan(first_pass, (zero_cols, zero_cols), (emb_blocks, view_blocks, scale_blocks))
    row_mass = row_mass.reshape(ROWS)
    row_weight = row_weight.reshape(ROWS)

    def column_pass(row_dual):
        dual_blocks = row_dual.reshape(N_ROW, ROWS_DEV)

        def add_block(running, blocks):
            emb_block, scale_block, dual_block = blocks
            return running + jnp.dot(dual_block, plan_block(emb_block, scale_block), precision=lax.Precision.HIGHEST), None

        summed, unused = lax.scan(add_block, zero_cols, (emb_blocks, scale_blocks, dual_blocks))
        return summed

    def row_pass(col_dual):
        def one_block(blocks):
            emb_block, scale_block = blocks
            return jnp.dot(plan_block(emb_block, scale_block), col_dual, precision=lax.Precision.HIGHEST)

        return lax.map(one_block, (emb_blocks, scale_blocks)).reshape(ROWS)

    row_dual = row_weight / row_mass
    col_dual = (col_weight - column_pass(row_dual)) / col_mass
    for sweep in range(ITERS - 1):
        row_dual = (row_weight - row_pass(col_dual)) / row_mass
        col_dual = (col_weight - column_pass(row_dual)) / col_mass

    def final_pass(running, blocks):
        emb_block, view_block, scale_block, dual_block = blocks
        plan = plan_block(emb_block, scale_block)
        logit_grad = plan * (cot_block(view_block) - dual_block[:, None] - col_dual[None, :])
        scaled_grad = lax.optimization_barrier((logit_scale * logit_grad).astype(jnp.bfloat16)).astype(jnp.float32)
        scaled_plan = lax.optimization_barrier((-view_scale * plan).astype(jnp.bfloat16)).astype(jnp.float32)
        embed_part = jnp.dot(scaled_grad, proto_wide)
        proto_part = jnp.dot(scaled_grad.T, emb_block.astype(jnp.float32)) + jnp.dot(scaled_plan.T, view_block.astype(jnp.float32))
        return running + proto_part, embed_part

    proto_grad, embed_parts = lax.scan(final_pass, jnp.zeros((PROTOS, D), jnp.float32), (emb_blocks, view_blocks, scale_blocks, row_dual.reshape(N_ROW, ROWS_DEV)))
    return embed_parts.reshape(ROWS, D), proto_grad
```

```python
import functools

import jax
import jax.numpy as jnp
from jax import lax
from jax.experimental import pallas as pl
from jax.experimental.pallas import tpu as pltpu
from jax.sharding import PartitionSpec as P

ITERS = 4
LANES = 128
MESH = pl.DeviceIdType.MESH
F32 = jnp.float32
BF16 = jnp.bfloat16

DIMS = (4, 2, 2, 4, 8)


def dot_nt(left, right):
    return lax.dot_general(left, right, (((1,), (1,)), ((), ())), preferred_element_type=F32)


def dot_tn(left, right):
    return lax.dot_general(left, right, (((0,), (0,)), ((), ())), preferred_element_type=F32)


def down(row, height=LANES):
    return jnp.broadcast_to(row, (height, LANES)).T


def fold(block):
    return block.reshape(block.shape[0] // 8, 8, LANES).sum(0)


def kernel(
    dims,
    proto_total,
    emb_in,
    view_in,
    pro_in,
    rs_in,
    cs_in,
    eg_ref,
    pg_ref,
    ev,
    pr,
    rs,
    cs,
    plan,
    cot,
    lg,
    grad,
    splan,
    tail,
    colm,
    colw,
    bx0,
    by0,
    bz0,
    bx,
    by,
    bz,
    eb,
    fy,
    fx_out,
    fx,
    pb,
    fz,
    local_sem,
    g_send,
    g_recv,
    r_send,
    r_recv,
    c_send,
    c_recv,
    x_send,
    y_send,
    z_send,
    z0_send,
    x_recv,
    y_recv,
    z_recv,
    fx_send,
    fy_send,
    fz_send,
    fx_recv,
    fy_recv,
    fz_recv,
):
    nx, nyl, nc, nyh, nz = dims
    ny, nxc = nyl * nyh, nx * nc
    row_id, proto_id = lax.axis_index("row"), lax.axis_index("proto")
    yh, z = row_id // nz, row_id % nz
    core = proto_id % nc
    yl = (proto_id // nc) % nyl
    x = proto_id // (nc * nyl)
    y = yh * nyl + yl
    xc = x * nc + core

    def at_z(other):
        return (yh * nz + other, proto_id)

    def at_y(other):
        return ((other // nyl) * nz + z, (x * nyl + other % nyl) * nc + core)

    def at_xc(other):
        return (row_id, ((other // nc) * nyl + yl) * nc + other % nc)

    chunks, groups = plan.shape[0] // LANES, plan.shape[1] // LANES
    per_block = chunks // nyh
    width = emb_in.shape[-1]
    logit_scale = 1.0 / (0.05 * width)
    view_scale = 1.0 / (0.1 * width)
    mass_inverse = 1.0 / (64.0 * proto_total)

    own = pl.ds(yh * per_block, per_block)
    loads = [
        pltpu.make_async_copy(emb_in, ev.at[0, own], local_sem.at[0]),
        pltpu.make_async_copy(view_in, ev.at[1, own], local_sem.at[1]),
        pltpu.make_async_copy(rs_in, rs.at[own], local_sem.at[2]),
        pltpu.make_async_copy(cs_in.at[yh], cs, local_sem.at[3]),
        pltpu.make_async_copy(pro_in.at[yh], pr, local_sem.at[4]),
    ]
    for load in loads:
        load.start()

    barrier = pltpu.get_barrier_semaphore()
    for step in range(1, nz):
        pl.semaphore_signal(barrier, inc=1, device_id=at_z((z + step) % nz), device_id_type=MESH)
    for step in range(1, ny):
        pl.semaphore_signal(barrier, inc=1, device_id=at_y((y + step) % ny), device_id_type=MESH)
    for step in range(1, nxc):
        pl.semaphore_signal(barrier, inc=1, device_id=at_xc((xc + step) % nxc), device_id_type=MESH)
    for load in loads:
        load.wait()
    pl.semaphore_wait(barrier, nz + ny + nxc - 3)

    sign = 2 * yl - 1
    blocks = []
    sends = []
    for step in range(1, nyh):
        target = (y + sign * step + ny) % ny
        source = (y + (sign if step % 2 else -sign) * step + ny) % ny
        there = pl.ds((source // nyl) * per_block, per_block)
        blocks.append((source // nyl, there))
        rows_out = pltpu.make_async_remote_copy(
            ev.at[core, own], ev.at[core, own], g_send.at[step], g_recv.at[step], at_y(target), MESH
        )
        scale_out = pltpu.make_async_remote_copy(
            rs.at[own], rs.at[own], r_send.at[step], r_recv.at[step], at_y(target), MESH
        )
        rows_out.start()
        scale_out.start()
        sends += [rows_out, scale_out]

    colm[...] = jnp.zeros_like(colm)
    colw[...] = jnp.zeros_like(colw)

    def first_chunk(i):
        rows = pl.ds(pl.multiple_of(i * LANES, LANES), LANES)
        lg[...] = dot_nt(ev[0, i], pr[...])
        cot[rows, :] = dot_nt(ev[1, i], pr[...]) * -view_scale
        scale = down(rs[i]) * mass_inverse
        mass = jnp.zeros((LANES, LANES), F32)
        weight = jnp.zeros((LANES, LANES), F32)
        for k in range(groups):
            cols = slice(k * LANES, (k + 1) * LANES)
            value = scale * cs[k : k + 1, :] * jnp.exp(lg[:, cols] * logit_scale)
            plan[rows, cols] = value
            weighted = value * cot[rows, cols]
            mass = mass + value
            weight = weight + weighted
            colm[k] += fold(value)
            colw[k] += fold(weighted)
        bx0[xc, 0, pl.ds(i, 1), :] = mass.T.sum(0, keepdims=True)
        bx0[xc, 1, pl.ds(i, 1), :] = weight.T.sum(0, keepdims=True)

    def first_block(block):
        @pl.loop(0, per_block)
        def _(part):
            first_chunk(block * per_block + part)

    first_block(yh)
    partner = at_xc(x * nc + (core + 1) % nc)
    for step, (block, there) in enumerate(blocks, 1):
        pltpu.make_async_remote_copy(
            ev.at[core, there], ev.at[core, there], g_send.at[step], g_recv.at[step], partner, MESH
        ).wait_recv()
        hand = pltpu.make_async_remote_copy(
            ev.at[core, there], ev.at[core, there], c_send.at[step], c_recv.at[step], partner, MESH
        )
        hand.start()
        sends.append(hand)
        pltpu.make_async_remote_copy(
            rs.at[there], rs.at[there], r_send.at[step], r_recv.at[step], partner, MESH
        ).wait_recv()
        taken = ev.at[(core + 1) % nc, there]
        pltpu.make_async_remote_copy(
            taken, taken, c_send.at[step], c_recv.at[step], partner, MESH
        ).wait_recv()
        first_block(block)

    def start(slots, me, count, address, send, recv):
        for step in range(1, count):
            other = (me + step) % count
            pltpu.make_async_remote_copy(
                slots.at[me], slots.at[me], send.at[step], recv.at[me], address(other), MESH
            ).start()

    def finish(slots, me, count, address, send, recv):
        for step in range(1, count):
            other = (me + step) % count
            pltpu.make_async_remote_copy(
                slots.at[other], slots.at[other], send.at[step], recv.at[other], address(other), MESH
            ).wait_recv()
        for step in range(1, count):
            other = (me + step) % count
            pltpu.make_async_remote_copy(
                slots.at[me], slots.at[me], send.at[step], recv.at[me], address(other), MESH
            ).wait_send()

    def total(slots, count):
        result = slots[0]
        for slot in range(1, count):
            result = result + slots[slot]
        return result

    along_x = (xc, nxc, at_xc)
    along_y = (y, ny, at_y)
    along_z = (z, nz, at_z)

    start(bx0, *along_x, x_send, x_recv.at[0])
    for k in range(groups):
        bz0[z, 0, k : k + 1, :] = colm[k].sum(0, keepdims=True)
        bz0[z, 1, k : k + 1, :] = colw[k].sum(0, keepdims=True)
    start(bz0, *along_z, z0_send, z_recv.at[0])

    @pl.loop(0, chunks)
    def _(i):
        rows = pl.ds(pl.multiple_of(i * LANES, LANES), LANES)
        splan[rows, :] = (plan[rows, :] * -view_scale).astype(BF16)

    finish(bx0, *along_x, x_send, x_recv.at[0])
    by0[y] = total(bx0, nxc)
    start(by0, *along_y, y_send, y_recv.at[0])

    @pl.loop(0, groups)
    def _(k):
        cols = pl.ds(pl.multiple_of(k * LANES, LANES), LANES)
        tail[cols, :] = dot_tn(splan[:, cols], ev[1].reshape(chunks * LANES, width))

    finish(by0, *along_y, y_send, y_recv.at[0])
    row_sums = total(by0, ny)
    row_mass, row_weight = row_sums[0], row_sums[1]

    def column_part(row_dual, k):
        bx[k, xc] = row_dual
        tiles = tuple(jnp.zeros((8, LANES), F32) for _ in range(groups))

        def add(i, tiles):
            rows = pl.ds(pl.multiple_of(i * LANES, LANES), LANES)
            dual = down(bx[k, xc, pl.ds(i, 1), :])
            return tuple(
                tile + fold(plan[rows, g * LANES : (g + 1) * LANES] * dual)
                for g, tile in enumerate(tiles)
            )

        tiles = lax.fori_loop(0, chunks, add, tiles)
        for g, tile in enumerate(tiles):
            bz[k, z, g : g + 1, :] = tile.sum(0, keepdims=True)

    def row_part(col_dual, k):
        def one(i, unused):
            rows = pl.ds(pl.multiple_of(i * LANES, LANES), LANES)
            block = plan[rows, :LANES] * col_dual[0:1, :]
            for g in range(1, groups):
                block = block + plan[rows, g * LANES : (g + 1) * LANES] * col_dual[g : g + 1, :]
            bx[k, xc, pl.ds(i, 1), :] = block.T.sum(0, keepdims=True)
            return unused

        lax.fori_loop(0, chunks, one, 0)

    row_dual = row_weight / row_mass
    column_part(row_dual, ITERS - 1)
    start(bz.at[ITERS - 1], *along_z, z_send, z_recv.at[ITERS])
    finish(bz0, *along_z, z0_send, z_recv.at[0])
    col_sums = total(bz0, nz)
    col_mass, col_weight = col_sums[0], col_sums[1]
    finish(bz.at[ITERS - 1], *along_z, z_send, z_recv.at[ITERS])
    col_dual = (col_weight - total(bz.at[ITERS - 1], nz)) / col_mass

    def sweep(k, duals):
        row_part(duals[1], k)
        start(bx.at[k], *along_x, x_send, x_recv.at[k + 1])
        finish(bx.at[k], *along_x, x_send, x_recv.at[k + 1])
        by[k, y] = total(bx.at[k], nxc)
        start(by.at[k], *along_y, y_send, y_recv.at[k + 1])
        finish(by.at[k], *along_y, y_send, y_recv.at[k + 1])
        row_dual = (row_weight - total(by.at[k], ny)) / row_mass
        column_part(row_dual, k)
        start(bz.at[k], *along_z, z_send, z_recv.at[k + 1])
        finish(bz.at[k], *along_z, z_send, z_recv.at[k + 1])
        return row_dual, (col_weight - total(bz.at[k], nz)) / col_mass

    row_dual, col_dual = lax.fori_loop(0, ITERS - 1, sweep, (row_dual, col_dual))

    bx[0, xc] = row_dual
    half = nx // per_block

    def last_chunk(i, part, block):
        rows = pl.ds(pl.multiple_of(i * LANES, LANES), LANES)
        dual = down(bx[0, xc, pl.ds(i, 1), :])
        for g in range(groups):
            cols = slice(g * LANES, (g + 1) * LANES)
            piece = plan[rows, cols] * (cot[rows, cols] - dual - col_dual[g : g + 1, :])
            grad[rows, cols] = (logit_scale * piece).astype(BF16)
        product = jnp.dot(grad[rows, :], pr[...], preferred_element_type=F32)
        eb[block, pl.ds(part * half, half)] = product.reshape(
            half, nyl, LANES // (half * nyl), LANES
        ).astype(BF16)

    def send_rows(other, step):
        return pltpu.make_async_remote_copy(
            eb.at[other // nyl, :, other % nyl],
            fy.at[y],
            fy_send.at[step],
            fy_recv.at[y],
            at_y(other),
            MESH,
        )

    row_sends = []
    for step in range(1, nyh + 1):
        block = (yh + step) % nyh

        @pl.loop(0, per_block)
        def _(part):
            last_chunk(block * per_block + part, part, block)

        for low in range(nyl):
            if step < nyh:
                other, slot = block * nyl + low, step * nyl + low
            elif low:
                other, slot = yh * nyl + (yl + low) % nyl, low
            else:
                continue
            row_sends.append(send_rows(other, slot))
            row_sends[-1].start()

    proto_sends = []
    for step in range(1, nz + 1):
        other = (z + step) % nz
        cols = pl.ds(pl.multiple_of(other * LANES, LANES), LANES)
        share = tail[cols, :] + dot_tn(grad[:, cols], ev[0].reshape(chunks * LANES, width))
        if step < nz:
            pb[step] = share.astype(BF16)
            proto_sends.append(
                pltpu.make_async_remote_copy(
                    pb.at[step], fz.at[z], fz_send.at[step], fz_recv.at[z], at_z(other), MESH
                )
            )
            proto_sends[-1].start()
        else:
            pg_ref[...] = share

    def arrived(slots, me, count, recv, send, address):
        for step in range(1, count):
            other = (me + step) % count
            pltpu.make_async_remote_copy(
                slots.at[other], slots.at[other], send.at[step], recv.at[other], address(other), MESH
            ).wait_recv()

    arrived(fy, y, ny, fy_recv, fy_send, at_y)
    rows_sum = eb[yh, :, yl].astype(F32)
    for step in range(1, ny):
        rows_sum = rows_sum + fy[(y + step) % ny].astype(F32)
    fx_out[...] = rows_sum.reshape(fx_out.shape)
    last_sends = []
    for step in range(1, nxc):
        other = (xc + step) % nxc
        last_sends.append(
            pltpu.make_async_remote_copy(
                fx_out.at[other], fx.at[xc], fx_send.at[step], fx_recv.at[xc], at_xc(other), MESH
            )
        )
        last_sends[-1].start()

    arrived(fz, z, nz, fz_recv, fz_send, at_z)
    share = pg_ref[...]
    for step in range(1, nz):
        share = share + fz[(z + step) % nz].astype(F32)
    pg_ref[...] = share

    arrived(fx, xc, nxc, fx_recv, fx_send, at_xc)
    rows_out = fx_out[xc]
    for step in range(1, nxc):
        rows_out = rows_out + fx[(xc + step) % nxc]
    eg_ref[...] = rows_out

    for send in sends + row_sends + proto_sends + last_sends:
        send.wait_send()


def build(mesh, dims):
    nx, nyl, nc, nyh, nz = dims
    ny, nxc = nyl * nyh, nx * nc

    def per_device(embeddings, second_view, prototypes, row_scale, col_scale):
        row_count, width = embeddings.shape
        proto_count = prototypes.shape[0]
        proto_total = proto_count * nx * nyl * nc
        rows, cols = row_count * nyh, proto_count // nyh
        per_block = row_count // LANES
        chunks, groups = rows // LANES, cols // LANES
        rows_out, cols_out = row_count // (nx * nyl * nc), cols // nz
        dma = pltpu.SemaphoreType.DMA
        scratch = [
            pltpu.VMEM((2, chunks, LANES, width), BF16),
            pltpu.VMEM((cols, width), BF16),
            pltpu.VMEM((chunks, 1, LANES), F32),
            pltpu.VMEM((groups, LANES), F32),
            pltpu.VMEM((rows, cols), F32),
            pltpu.VMEM((rows, cols), F32),
            pltpu.VMEM((LANES, cols), F32),
            pltpu.VMEM((rows, cols), BF16),
            pltpu.VMEM((rows, cols), BF16),
            pltpu.VMEM((cols, width), F32),
            pltpu.VMEM((groups, 8, LANES), F32),
            pltpu.VMEM((groups, 8, LANES), F32),
            pltpu.VMEM((nxc, 2, chunks, LANES), F32),
            pltpu.VMEM((ny, 2, chunks, LANES), F32),
            pltpu.VMEM((nz, 2, groups, LANES), F32),
            pltpu.VMEM((ITERS, nxc, chunks, LANES), F32),
            pltpu.VMEM((ITERS, ny, chunks, LANES), F32),
            pltpu.VMEM((ITERS, nz, groups, LANES), F32),
            pltpu.VMEM((nyh, nx, nyl, nc * rows_out, width), BF16),
            pltpu.VMEM((ny, nx, nc * rows_out, width), BF16),
            pltpu.VMEM((nxc, rows_out, width), F32),
            pltpu.VMEM((nxc, rows_out, width), F32),
            pltpu.VMEM((nz, cols_out, width), BF16),
            pltpu.VMEM((nz, cols_out, width), BF16),
            dma((5,)),
            dma((nyh,)),
            dma((nyh,)),
            dma((nyh,)),
            dma((nyh,)),
            dma((nyh,)),
            dma((nyh,)),
            dma((nxc,)),
            dma((ny,)),
            dma((nz,)),
            dma((nz,)),
            dma((ITERS, nxc)),
            dma((ITERS, ny)),
            dma((ITERS + 1, nz)),
            dma((nxc,)),
            dma((ny,)),
            dma((nz,)),
            dma((nxc,)),
            dma((ny,)),
            dma((nz,)),
        ]
        return pl.pallas_call(
            functools.partial(kernel, dims, proto_total),
            out_shape=(
                jax.ShapeDtypeStruct((rows_out, width), F32),
                jax.ShapeDtypeStruct((cols_out, width), F32),
            ),
            in_specs=[pl.BlockSpec(memory_space=pl.ANY)] * 5,
            out_specs=(pl.BlockSpec(memory_space=pltpu.VMEM),) * 2,
            scratch_shapes=scratch,
            compiler_params=pltpu.CompilerParams(
                collective_id=0, has_side_effects=True, vmem_limit_bytes=48 * 1024 * 1024
            ),
        )(
            embeddings.reshape(per_block, LANES, width),
            second_view.reshape(per_block, LANES, width),
            prototypes.reshape(nyh, cols, width),
            row_scale.reshape(per_block, 1, LANES),
            col_scale.reshape(nyh, groups, LANES),
        )

    return jax.shard_map(
        per_device,
        mesh=mesh,
        in_specs=(P("row", None), P("row", None), P("proto", None), P("row"), P("proto")),
        out_specs=(P(("row", "proto"), None), P(("proto", "row"), None)),
        check_vma=False,
    )


def solution(mesh):
    return build(mesh, DIMS)
```

```python
import functools
from types import SimpleNamespace

import jax
import jax.numpy as jnp
from jax import lax
from jax.experimental import pallas as pl
from jax.experimental.pallas import tpu as pltpu
from jax.sharding import PartitionSpec as P

ITERS = 4
LANES = 128
MESH = pl.DeviceIdType.MESH
F32 = jnp.float32
BF16 = jnp.bfloat16

DIMS = (4, 2, 2, 4, 8)


def dot_nt(left, right):
    return lax.dot_general(left, right, (((1,), (1,)), ((), ())), preferred_element_type=F32)


def dot_tn(left, right):
    return lax.dot_general(left, right, (((0,), (0,)), ((), ())), preferred_element_type=F32)


def down(row):
    return jnp.broadcast_to(row, (LANES, LANES)).T


def fold(block):
    return block.reshape(block.shape[0] // 8, 8, LANES).sum(0)


def across(block):
    return block.T.sum(0, keepdims=True)


def tiles_of(count, start=0):
    return [slice((start + g) * LANES, (start + g + 1) * LANES) for g in range(count)]


def aligned(i, size=LANES):
    return pl.ds(pl.multiple_of(i * size, size), size)


def kernel(dims, proto_total, names, emb_in, view_in, pro_in, rs_in, cs_in, eg_ref, pg_ref, *scratch):
    m = SimpleNamespace(**dict(zip(names, scratch)))
    nx, nyl, nc, nyh, nz = dims
    ny, nxc, npr = nyl * nyh, nx * nc, nx * nyl * nc
    row_id, me_p = lax.axis_index("row"), lax.axis_index("proto")
    yh, z = row_id // nz, row_id % nz
    core = me_p % nc
    yl = (me_p // nc) % nyl
    x = me_p // (nc * nyl)
    y = yh * nyl + yl
    xc = x * nc + core

    def at_z(other):
        return (yh * nz + other, me_p)

    def at_yh(other):
        return (other * nz + z, me_p)

    def at_y(other):
        return ((other // nyl) * nz + z, (x * nyl + other % nyl) * nc + core)

    def at_xc(other):
        return (row_id, ((other // nc) * nyl + yl) * nc + other % nc)

    def at_p(other):
        return (row_id, other)

    chunks, groups = m.plan.shape[0] // LANES, m.plan.shape[1] // LANES
    per_block = chunks // nyh
    width = emb_in.shape[-1]
    logit_scale = 1.0 / (0.05 * width)
    view_scale = 1.0 / (0.1 * width)
    mass_inverse = 1.0 / (64.0 * proto_total)

    own = pl.ds(yh * per_block, per_block)
    small_loads = [
        pltpu.make_async_copy(emb_in, m.ev.at[0, own], m.local_sem.at[0]),
        pltpu.make_async_copy(view_in, m.ev.at[1, own], m.local_sem.at[1]),
        pltpu.make_async_copy(rs_in, m.rs.at[own], m.local_sem.at[2]),
        pltpu.make_async_copy(cs_in, m.cs, m.local_sem.at[3]),
    ]
    for load in small_loads:
        load.start()

    def pro_load(part):
        return pltpu.make_async_copy(pro_in.at[part], m.pr.at[part], m.pro_sem.at[part])

    for part in range(nyh):
        pro_load(part).start()

    barrier = pltpu.get_barrier_semaphore()
    for count, me, address in ((nz, z, at_z), (ny, y, at_y), (npr, me_p, at_p)):
        for step in range(1, count):
            pl.semaphore_signal(
                barrier, inc=1, device_id=address((me + step) % count), device_id_type=MESH
            )
    for load in small_loads:
        load.wait()

    m.colm[...] = jnp.zeros_like(m.colm)
    m.colw[...] = jnp.zeros_like(m.colw)
    m.rowm[...] = jnp.zeros_like(m.rowm)
    m.roww[...] = jnp.zeros_like(m.roww)

    def own_part(part, h):
        i = yh * per_block + h
        rows = aligned(h)
        m.lg[...] = dot_nt(m.ev[0, i], m.pr[part])
        m.cot0[part, rows, :] = dot_nt(m.ev[1, i], m.pr[part]) * -view_scale
        scale = down(m.rs[i]) * mass_inverse
        mass = m.rowm[h]
        weight = m.roww[h]
        for g, cols in enumerate(tiles_of(groups)):
            value = scale * m.cs[part, g : g + 1, :] * jnp.exp(m.lg[:, cols] * logit_scale)
            m.plan0[part, rows, cols] = value
            weighted = value * m.cot0[part, rows, cols]
            mass = mass + value
            weight = weight + weighted
            m.colm[part, g] += fold(value)
            m.colw[part, g] += fold(weighted)
        m.rowm[h] = mass
        m.roww[h] = weight

    def own_parts(first, last):
        @pl.loop(first, last)
        def _(part):
            pro_load(part).wait()

            @pl.loop(0, per_block)
            def _(h):
                own_part(part, h)

    own_parts(0, nyh // 2)
    pl.semaphore_wait(barrier, nz + ny + npr - 3)

    sign = 2 * yl - 1
    partner = at_xc(x * nc + (core + 1) % nc)
    blocks = []
    sends = []
    for step in range(1, nyh):
        target = (y + sign * step + ny) % ny
        source = (y + (sign if step % 2 else -sign) * step + ny) % ny
        blocks.append((source // nyl, pl.ds((source // nyl) * per_block, per_block)))
        rows_out = pltpu.make_async_remote_copy(
            m.ev.at[core, own], m.ev.at[core, own], m.g_send.at[step], m.g_recv.at[step], at_y(target), MESH
        )
        scale_out = pltpu.make_async_remote_copy(
            m.rs.at[own], m.rs.at[own], m.r_send.at[step], m.r_recv.at[step], at_y(target), MESH
        )
        rows_out.start()
        scale_out.start()
        sends += [rows_out, scale_out]

    own_parts(nyh // 2, nyh)

    def start(slots, me, count, address, send, recv):
        for step in range(1, count):
            other = (me + step) % count
            pltpu.make_async_remote_copy(
                slots.at[me], slots.at[me], send.at[step], recv.at[me], address(other), MESH
            ).start()

    def finish(slots, me, count, address, send, recv):
        for step in range(1, count):
            other = (me + step) % count
            pltpu.make_async_remote_copy(
                slots.at[other], slots.at[other], send.at[step], recv.at[other], address(other), MESH
            ).wait_recv()
        for step in range(1, count):
            other = (me + step) % count
            pltpu.make_async_remote_copy(
                slots.at[me], slots.at[me], send.at[step], recv.at[me], address(other), MESH
            ).wait_send()

    def scatter(shares, slots, me, count, address, send, recv):
        copies = []
        for step in range(1, count):
            other = (me + step) % count
            copies.append(
                pltpu.make_async_remote_copy(
                    shares.at[other], slots.at[me], send.at[step], recv.at[me], address(other), MESH
                )
            )
            copies[-1].start()
        return copies

    def arrived(slots, me, count, address, send, recv):
        for step in range(1, count):
            other = (me + step) % count
            pltpu.make_async_remote_copy(
                slots.at[other], slots.at[other], send.at[step], recv.at[other], address(other), MESH
            ).wait_recv()

    def total(slots, count):
        result = slots[0]
        for slot in range(1, count):
            result = result + slots[slot]
        return result

    along_x = (xc, nxc, at_xc)
    along_y = (y, ny, at_y)
    along_z = (z, nz, at_z)
    along_p = (me_p, npr, at_p)
    along_h = (yh, nyh, at_yh)

    for h in range(per_block):
        m.bw[me_p, h : h + 1, :] = across(m.rowm[h])
        m.bw[me_p, per_block + h : per_block + h + 1, :] = across(m.roww[h])
    start(m.bw, *along_p, m.w_send, m.w_recv)

    own_rows = aligned(yh, per_block * LANES)
    moves = [
        pltpu.make_async_copy(m.plan0.at[yh], m.plan.at[own_rows], m.local_sem.at[0]),
        pltpu.make_async_copy(m.cot0.at[yh], m.cot.at[own_rows], m.local_sem.at[1]),
    ]
    for move in moves:
        move.start()

    for part in range(nyh):
        for g in range(groups):
            m.cms[part, 0, g : g + 1, :] = m.colm[part, g].sum(0, keepdims=True)
            m.cms[part, 1, g : g + 1, :] = m.colw[part, g].sum(0, keepdims=True)
    sends += scatter(m.cms, m.cmr, *along_h, m.cm_send, m.cm_recv)
    m.cmr[yh] = m.cms[yh]

    finish(m.bw, *along_p, m.w_send, m.w_recv)
    sums = total(m.bw, npr)
    m.rsum[yh] = sums
    m.dual0[...] = sums[per_block:] / sums[:per_block]
    start(m.rsum, *along_h, m.q_send, m.q_recv)

    @pl.loop(0, nyh)
    def _(part):
        found = [jnp.zeros((8, LANES), F32)] * groups
        for h in range(per_block):
            dual = down(m.dual0[h : h + 1, :])
            for g, cols in enumerate(tiles_of(groups)):
                found[g] = found[g] + fold(m.plan0[part, h * LANES : (h + 1) * LANES, cols] * dual)
        for g in range(groups):
            m.cps[part, g : g + 1, :] = found[g].sum(0, keepdims=True)

    sends += scatter(m.cps, m.cpr, *along_h, m.cp_send, m.cp_recv)
    m.cpr[yh] = m.cps[yh]

    for step, (block, there) in enumerate(blocks, 1):
        mine = m.ev.at[core, there]
        pltpu.make_async_remote_copy(
            mine, mine, m.g_send.at[step], m.g_recv.at[step], partner, MESH
        ).wait_recv()
        hand = pltpu.make_async_remote_copy(
            mine, mine, m.c_send.at[step], m.c_recv.at[step], partner, MESH
        )
        hand.start()
        sends.append(hand)

    arrived(m.cmr, *along_h, m.cm_send, m.cm_recv)
    m.bz0[z] = total(m.cmr, nyh)
    start(m.bz0, *along_z, m.z0_send, m.z_recv.at[0])

    def fill(step):
        block, there = blocks[step - 1]
        taken = m.ev.at[(core + 1) % nc, there]
        scales = m.rs.at[there]
        pltpu.make_async_remote_copy(
            scales, scales, m.r_send.at[step], m.r_recv.at[step], partner, MESH
        ).wait_recv()
        pltpu.make_async_remote_copy(
            taken, taken, m.c_send.at[step], m.c_recv.at[step], partner, MESH
        ).wait_recv()

        @pl.loop(0, per_block)
        def _(h):
            i = block * per_block + h
            rows = aligned(i)
            m.lg[...] = dot_nt(m.ev[0, i], m.pr[yh])
            m.cot[rows, :] = dot_nt(m.ev[1, i], m.pr[yh]) * -view_scale
            scale = down(m.rs[i]) * mass_inverse
            for g, cols in enumerate(tiles_of(groups)):
                m.plan[rows, cols] = (
                    scale * m.cs[yh, g : g + 1, :] * jnp.exp(m.lg[:, cols] * logit_scale)
                )

    fill(1)
    arrived(m.cpr, *along_h, m.cp_send, m.cp_recv)
    m.bz[ITERS - 1, z] = total(m.cpr, nyh)
    start(m.bz.at[ITERS - 1], *along_z, m.z_send, m.z_recv.at[ITERS])
    for step in range(2, nyh):
        fill(step)
    finish(m.rsum, *along_h, m.q_send, m.q_recv)
    for block in range(nyh):
        place = slice(block * per_block, (block + 1) * per_block)
        m.row_mass[place, :] = m.rsum[block, :per_block, :]
        m.row_weight[place, :] = m.rsum[block, per_block:, :]
    for move in moves:
        move.wait()
    finish(m.bz0, *along_z, m.z0_send, m.z_recv.at[0])
    col_sums = total(m.bz0, nz)
    col_mass, col_weight = col_sums[0], col_sums[1]
    finish(m.bz.at[ITERS - 1], *along_z, m.z_send, m.z_recv.at[ITERS])
    col_dual = (col_weight - total(m.bz.at[ITERS - 1], nz)) / col_mass

    def column_part(row_dual, k):
        m.bx[k, xc] = row_dual
        found = tuple(jnp.zeros((8, LANES), F32) for _ in range(groups))

        def add(i, found):
            rows = aligned(i)
            dual = down(m.bx[k, xc, pl.ds(i, 1), :])
            return tuple(
                tile + fold(m.plan[rows, cols] * dual)
                for tile, cols in zip(found, tiles_of(groups))
            )

        found = lax.fori_loop(0, chunks, add, found)
        for g, tile in enumerate(found):
            m.bz[k, z, g : g + 1, :] = tile.sum(0, keepdims=True)

    def row_part(col_dual, k):
        @pl.loop(0, chunks)
        def _(i):
            rows = aligned(i)
            block = m.plan[rows, :LANES] * col_dual[0:1, :]
            for g, cols in enumerate(tiles_of(groups - 1, 1), 1):
                block = block + m.plan[rows, cols] * col_dual[g : g + 1, :]
            m.bx[k, xc, pl.ds(i, 1), :] = across(block)

    def sweep(k, duals):
        row_part(duals[1], k)
        start(m.bx.at[k], *along_x, m.x_send, m.x_recv.at[k])

        @pl.when(k == 0)
        def _():
            @pl.loop(0, chunks)
            def _(i):
                rows = aligned(i)
                m.splan[rows, :] = (m.plan[rows, :] * -view_scale).astype(BF16)

        finish(m.bx.at[k], *along_x, m.x_send, m.x_recv.at[k])
        m.by[k, y] = total(m.bx.at[k], nxc)
        start(m.by.at[k], *along_y, m.y_send, m.y_recv.at[k])

        @pl.when(k == 0)
        def _():
            @pl.loop(0, groups)
            def _(g):
                cols = aligned(g)
                m.tail[cols, :] = dot_tn(m.splan[:, cols], m.ev[1].reshape(chunks * LANES, width))

        finish(m.by.at[k], *along_y, m.y_send, m.y_recv.at[k])
        row_dual = (m.row_weight[...] - total(m.by.at[k], ny)) / m.row_mass[...]
        column_part(row_dual, k)
        start(m.bz.at[k], *along_z, m.z_send, m.z_recv.at[k + 1])
        finish(m.bz.at[k], *along_z, m.z_send, m.z_recv.at[k + 1])
        return row_dual, (col_weight - total(m.bz.at[k], nz)) / col_mass

    row_dual, col_dual = lax.fori_loop(
        0, ITERS - 1, sweep, (jnp.zeros((chunks, LANES), F32), col_dual)
    )

    m.bx[0, xc] = row_dual
    half = nx // per_block

    def last_chunk(block, h):
        i = block * per_block + h
        rows = aligned(i)
        dual = down(m.bx[0, xc, pl.ds(i, 1), :])
        for g, cols in enumerate(tiles_of(groups)):
            piece = m.plan[rows, cols] * (m.cot[rows, cols] - dual - col_dual[g : g + 1, :])
            m.grad[rows, cols] = (logit_scale * piece).astype(BF16)
        product = jnp.dot(m.grad[rows, :], m.pr[yh], preferred_element_type=F32)
        m.eb[block, pl.ds(h * half, half)] = product.reshape(
            half, nyl, nc, LANES // (half * nyl * nc), width
        ).astype(BF16)

    for step in range(1, nyh + 1):
        block = (yh + step) % nyh

        @pl.loop(0, per_block)
        def _(h):
            last_chunk(block, h)

        for turn in range(1, nxc):
            other = (xc + turn) % nxc
            sends.append(
                pltpu.make_async_remote_copy(
                    m.eb.at[block, other // nc, :, other % nc],
                    m.fx.at[block, xc],
                    m.fx_send.at[step - 1, turn],
                    m.fx_recv.at[block, xc],
                    at_xc(other),
                    MESH,
                )
            )
            sends[-1].start()

    for step in range(1, nz + 1):
        other = (z + step) % nz
        cols = aligned(other)
        share = m.tail[cols, :] + dot_tn(m.grad[:, cols], m.ev[0].reshape(chunks * LANES, width))
        if step < nz:
            m.pb[step] = share.astype(BF16)
            sends.append(
                pltpu.make_async_remote_copy(
                    m.pb.at[step], m.fz.at[z], m.fz_send.at[step], m.fz_recv.at[z], at_z(other), MESH
                )
            )
            sends[-1].start()
        else:
            pg_ref[...] = share

    for step in range(1, nyh + 1):
        block = (yh + step) % nyh
        arrived(m.fx.at[block], *along_x, m.fx_send.at[step - 1], m.fx_recv.at[block])
        part = m.eb[block, x, :, core].astype(F32)
        for turn in range(1, nxc):
            part = part + m.fx[block, (xc + turn) % nxc].astype(F32)
        m.fy_out[pl.ds(block * nyl, nyl)] = part
        for low in range(nyl):
            if step < nyh:
                other, slot = block * nyl + low, (step - 1) * nyl + low
            elif low:
                other, slot = yh * nyl + (yl + low) % nyl, (step - 1) * nyl + low
            else:
                continue
            sends.append(
                pltpu.make_async_remote_copy(
                    m.fy_out.at[other], m.fy.at[y], m.fy_send.at[slot], m.fy_recv.at[y], at_y(other), MESH
                )
            )
            sends[-1].start()

    arrived(m.fz, *along_z, m.fz_send, m.fz_recv)
    share = pg_ref[...]
    for step in range(1, nz):
        share = share + m.fz[(z + step) % nz].astype(F32)
    pg_ref[...] = share

    arrived(m.fy, *along_y, m.fy_send, m.fy_recv)
    rows_out = m.fy_out[y]
    for step in range(1, ny):
        rows_out = rows_out + m.fy[(y + step) % ny]
    eg_ref[...] = rows_out

    for send in sends:
        send.wait_send()


def build(mesh, dims):
    nx, nyl, nc, nyh, nz = dims
    ny, nxc, npr = nyl * nyh, nx * nc, nx * nyl * nc

    def per_device(embeddings, second_view, prototypes, row_scale, col_scale):
        row_count, width = embeddings.shape
        proto_count = prototypes.shape[0]
        proto_total = proto_count * npr
        rows, cols = row_count * nyh, proto_count // nyh
        per_block = row_count // LANES
        chunks, groups = rows // LANES, cols // LANES
        rows_out, cols_out = row_count // npr, cols // nz
        vmem, dma = pltpu.VMEM, pltpu.SemaphoreType.DMA
        scratch = dict(
            ev=vmem((2, chunks, LANES, width), BF16),
            pr=vmem((nyh, cols, width), BF16),
            rs=vmem((chunks, 1, LANES), F32),
            cs=vmem((nyh, groups, LANES), F32),
            plan0=vmem((nyh, row_count, cols), F32),
            cot0=vmem((nyh, row_count, cols), F32),
            plan=vmem((rows, cols), F32),
            cot=vmem((rows, cols), F32),
            lg=vmem((LANES, cols), F32),
            grad=vmem((rows, cols), BF16),
            splan=vmem((rows, cols), BF16),
            tail=vmem((cols, width), F32),
            colm=vmem((nyh, groups, 8, LANES), F32),
            colw=vmem((nyh, groups, 8, LANES), F32),
            rowm=vmem((per_block, LANES, LANES), F32),
            roww=vmem((per_block, LANES, LANES), F32),
            bw=vmem((npr, 2 * per_block, LANES), F32),
            rsum=vmem((nyh, 2 * per_block, LANES), F32),
            dual0=vmem((per_block, LANES), F32),
            row_mass=vmem((chunks, LANES), F32),
            row_weight=vmem((chunks, LANES), F32),
            cms=vmem((nyh, 2, groups, LANES), F32),
            cmr=vmem((nyh, 2, groups, LANES), F32),
            cps=vmem((nyh, groups, LANES), F32),
            cpr=vmem((nyh, groups, LANES), F32),
            bz0=vmem((nz, 2, groups, LANES), F32),
            bx=vmem((ITERS - 1, nxc, chunks, LANES), F32),
            by=vmem((ITERS - 1, ny, chunks, LANES), F32),
            bz=vmem((ITERS, nz, groups, LANES), F32),
            eb=vmem((nyh, nx, nyl, nc, rows_out, width), BF16),
            fx=vmem((nyh, nxc, nyl, rows_out, width), BF16),
            fy_out=vmem((ny, rows_out, width), F32),
            fy=vmem((ny, rows_out, width), F32),
            pb=vmem((nz, cols_out, width), BF16),
            fz=vmem((nz, cols_out, width), BF16),
            local_sem=dma((4,)),
            pro_sem=dma((nyh,)),
            g_send=dma((nyh,)),
            g_recv=dma((nyh,)),
            r_send=dma((nyh,)),
            r_recv=dma((nyh,)),
            c_send=dma((nyh,)),
            c_recv=dma((nyh,)),
            w_send=dma((npr,)),
            w_recv=dma((npr,)),
            q_send=dma((nyh,)),
            q_recv=dma((nyh,)),
            cm_send=dma((nyh,)),
            cm_recv=dma((nyh,)),
            cp_send=dma((nyh,)),
            cp_recv=dma((nyh,)),
            x_send=dma((nxc,)),
            y_send=dma((ny,)),
            z_send=dma((nz,)),
            z0_send=dma((nz,)),
            x_recv=dma((ITERS - 1, nxc)),
            y_recv=dma((ITERS - 1, ny)),
            z_recv=dma((ITERS + 1, nz)),
            fx_send=dma((nyh, nxc)),
            fx_recv=dma((nyh, nxc)),
            fy_send=dma((ny,)),
            fy_recv=dma((ny,)),
            fz_send=dma((nz,)),
            fz_recv=dma((nz,)),
        )
        return pl.pallas_call(
            functools.partial(kernel, dims, proto_total, tuple(scratch)),
            out_shape=(
                jax.ShapeDtypeStruct((rows_out, width), F32),
                jax.ShapeDtypeStruct((cols_out, width), F32),
            ),
            in_specs=[pl.BlockSpec(memory_space=pltpu.HBM)] * 5,
            out_specs=(pl.BlockSpec(memory_space=pltpu.VMEM),) * 2,
            scratch_shapes=list(scratch.values()),
            compiler_params=pltpu.CompilerParams(
                collective_id=0, has_side_effects=True, vmem_limit_bytes=60 * 1024 * 1024
            ),
        )(
            embeddings.reshape(per_block, LANES, width),
            second_view.reshape(per_block, LANES, width),
            prototypes.reshape(nyh, cols, width),
            row_scale.reshape(per_block, 1, LANES),
            col_scale.reshape(nyh, groups, LANES),
        )

    return jax.shard_map(
        per_device,
        mesh=mesh,
        in_specs=(P("row", None), P("row", None), P("proto", None), P("row"), P("proto")),
        out_specs=(P(("row", "proto"), None), P(("proto", "row"), None)),
        check_vma=False,
    )


def solution(mesh):
    return build(mesh, DIMS)
```

```python
import functools
import math
from types import SimpleNamespace

import jax
import jax.numpy as jnp
from jax import lax
from jax.experimental import pallas as pl
from jax.experimental.pallas import tpu as pltpu
from jax.sharding import PartitionSpec as P

ITERS = 4
LANES = 128
MESH = pl.DeviceIdType.MESH
F32 = jnp.float32
BF16 = jnp.bfloat16

DIMS = (4, 2, 2, 4, 8)


def dot_nt(left, right):
    return lax.dot_general(left, right, (((1,), (1,)), ((), ())), preferred_element_type=F32)


def dot_tn(left, right):
    return lax.dot_general(left, right, (((0,), (0,)), ((), ())), preferred_element_type=F32)


def down(row):
    return jnp.broadcast_to(row, (LANES, LANES)).T


def fold(block):
    return block.reshape(block.shape[0] // 8, 8, LANES).sum(0)


def across(block):
    return block.T.sum(0, keepdims=True)


def tiles_of(count, start=0):
    return [slice((start + g) * LANES, (start + g + 1) * LANES) for g in range(count)]


def aligned(i, size=LANES):
    return pl.ds(pl.multiple_of(i * size, size), size)


def kernel(dims, proto_total, names, emb_in, view_in, pro_in, rs_in, cs_in, eg_ref, pg_ref, *scratch):
    m = SimpleNamespace(**dict(zip(names, scratch)))
    nx, nyl, nc, nyh, nz = dims
    ny, nxc, npr = nyl * nyh, nx * nc, nx * nyl * nc
    row_id, me_p = lax.axis_index("row"), lax.axis_index("proto")
    yh, z = row_id // nz, row_id % nz
    core = me_p % nc
    yl = (me_p // nc) % nyl
    x = me_p // (nc * nyl)
    y = yh * nyl + yl
    xc = x * nc + core

    def at_z(other):
        return (yh * nz + other, me_p)

    def at_yh(other):
        return (other * nz + z, me_p)

    def at_y(other):
        return ((other // nyl) * nz + z, (x * nyl + other % nyl) * nc + core)

    def at_xc(other):
        return (row_id, ((other // nc) * nyl + yl) * nc + other % nc)

    def at_p(other):
        return (row_id, other)

    chunks, groups = m.plan.shape[0] // LANES, m.plan.shape[1] // LANES
    per_block = chunks // nyh
    width = emb_in.shape[-1]
    logit_scale = 1.0 / (0.05 * width)
    view_scale = 1.0 / (0.1 * width)
    mass_inverse = 1.0 / (64.0 * proto_total)
    exp2_scale = logit_scale * math.log2(math.e)

    own = pl.ds(yh * per_block, per_block)
    small_loads = [
        pltpu.make_async_copy(emb_in, m.ev.at[0, own], m.local_sem.at[0]),
        pltpu.make_async_copy(view_in, m.ev.at[1, own], m.local_sem.at[1]),
        pltpu.make_async_copy(rs_in, m.rs.at[own], m.local_sem.at[2]),
        pltpu.make_async_copy(cs_in, m.cs, m.local_sem.at[3]),
    ]
    for load in small_loads:
        load.start()

    def pro_load(part):
        return pltpu.make_async_copy(pro_in.at[part], m.pr.at[part], m.pro_sem.at[part])

    for part in range(nyh):
        pro_load(part).start()

    barrier = pltpu.get_barrier_semaphore()
    for count, me, address in ((nz, z, at_z), (ny, y, at_y), (npr, me_p, at_p)):
        for step in range(1, count):
            pl.semaphore_signal(
                barrier, inc=1, device_id=address((me + step) % count), device_id_type=MESH
            )
    for load in small_loads:
        load.wait()

    m.rowm[...] = jnp.zeros_like(m.rowm)
    m.roww[...] = jnp.zeros_like(m.roww)

    def own_part(part):
        for h in range(per_block):
            rows = slice(h * LANES, (h + 1) * LANES)
            scale = down(m.rs[yh * per_block + h]) * mass_inverse
            mass = m.rowm[h]
            weight = m.roww[h]
            for g, cols in enumerate(tiles_of(groups)):
                value = scale * m.cs[part, g : g + 1, :] * jnp.exp2(m.lg[part % 2, rows, cols] * exp2_scale)
                m.plan0[part, rows, cols] = value
                weighted = value * m.dot0[part, rows, cols]
                mass = mass + value
                weight = weight + weighted
                if h:
                    m.colm[part, g] += fold(value)
                    m.colw[part, g] += fold(weighted)
                else:
                    m.colm[part, g] = fold(value)
                    m.colw[part, g] = fold(weighted)
            m.rowm[h] = mass
            m.roww[h] = weight

    def block_rows(kind, block):
        place = pl.ds(block * per_block, per_block)
        return m.ev[kind, place].reshape(per_block * LANES, width)

    def own_parts(first, last):
        for part in range(first, last):
            pro_load(part).wait()
        for part in range(first, last):
            m.lg[part % 2] = dot_nt(block_rows(0, yh), m.pr[part])
            m.dot0[part] = dot_nt(block_rows(1, yh), m.pr[part])
            own_part(part)

    own_parts(0, nyh // 2)
    pl.semaphore_wait(barrier, nz + ny + npr - 3)

    sign = 2 * yl - 1
    partner = at_xc(x * nc + (core + 1) % nc)
    blocks = []
    sends = []
    for step in range(1, nyh):
        target = (y + sign * step + ny) % ny
        source = (y + (sign if step % 2 else -sign) * step + ny) % ny
        blocks.append((source // nyl, pl.ds((source // nyl) * per_block, per_block)))
        rows_out = pltpu.make_async_remote_copy(
            m.ev.at[core, own], m.ev.at[core, own], m.g_send.at[step], m.g_recv.at[step], at_y(target), MESH
        )
        scale_out = pltpu.make_async_remote_copy(
            m.rs.at[own], m.rs.at[own], m.r_send.at[step], m.r_recv.at[step], at_y(target), MESH
        )
        rows_out.start()
        scale_out.start()
        sends += [rows_out, scale_out]

    own_parts(nyh // 2, nyh)

    def start(slots, me, count, address, send, recv):
        for step in range(1, count):
            other = (me + step) % count
            pltpu.make_async_remote_copy(
                slots.at[me], slots.at[me], send.at[step], recv.at[me], address(other), MESH
            ).start()

    def finish(slots, me, count, address, send, recv):
        for step in range(1, count):
            other = (me + step) % count
            pltpu.make_async_remote_copy(
                slots.at[other], slots.at[other], send.at[step], recv.at[other], address(other), MESH
            ).wait_recv()
        for step in range(1, count):
            other = (me + step) % count
            pltpu.make_async_remote_copy(
                slots.at[me], slots.at[me], send.at[step], recv.at[me], address(other), MESH
            ).wait_send()

    def scatter(shares, slots, me, count, address, send, recv):
        copies = []
        for step in range(1, count):
            other = (me + step) % count
            copies.append(
                pltpu.make_async_remote_copy(
                    shares.at[other], slots.at[me], send.at[step], recv.at[me], address(other), MESH
                )
            )
            copies[-1].start()
        return copies

    def arrived(slots, me, count, address, send, recv):
        for step in range(1, count):
            other = (me + step) % count
            pltpu.make_async_remote_copy(
                slots.at[other], slots.at[other], send.at[step], recv.at[other], address(other), MESH
            ).wait_recv()

    def total(slots, count):
        result = slots[0]
        for slot in range(1, count):
            result = result + slots[slot]
        return result

    along_x = (xc, nxc, at_xc)
    along_y = (y, ny, at_y)
    along_z = (z, nz, at_z)
    along_p = (me_p, npr, at_p)
    along_h = (yh, nyh, at_yh)

    for h in range(per_block):
        m.bw[me_p, h : h + 1, :] = across(m.rowm[h])
        m.bw[me_p, per_block + h : per_block + h + 1, :] = across(m.roww[h])
    start(m.bw, *along_p, m.w_send, m.w_recv)

    own_rows = aligned(yh, per_block * LANES)
    moves = [
        pltpu.make_async_copy(m.plan0.at[yh], m.plan.at[own_rows], m.local_sem.at[0]),
        pltpu.make_async_copy(m.dot0.at[yh], m.dot.at[own_rows], m.local_sem.at[1]),
    ]
    for move in moves:
        move.start()

    for part in range(nyh):
        for g in range(groups):
            m.cms[part, 0, g : g + 1, :] = m.colm[part, g].sum(0, keepdims=True)
            m.cms[part, 1, g : g + 1, :] = m.colw[part, g].sum(0, keepdims=True)
    sends += scatter(m.cms, m.cmr, *along_h, m.cm_send, m.cm_recv)
    m.cmr[yh] = m.cms[yh]

    finish(m.bw, *along_p, m.w_send, m.w_recv)
    sums = total(m.bw, npr)
    m.rsum[yh] = sums
    m.dual0[...] = sums[per_block:] * -view_scale / sums[:per_block]
    start(m.rsum, *along_h, m.q_send, m.q_recv)

    for part in range(nyh):
        found = [jnp.zeros((8, LANES), F32)] * groups
        for h in range(per_block):
            dual = down(m.dual0[h : h + 1, :])
            for g, cols in enumerate(tiles_of(groups)):
                found[g] = found[g] + fold(m.plan0[part, h * LANES : (h + 1) * LANES, cols] * dual)
        for g in range(groups):
            m.cps[part, g : g + 1, :] = found[g].sum(0, keepdims=True)

    sends += scatter(m.cps, m.cpr, *along_h, m.cp_send, m.cp_recv)
    m.cpr[yh] = m.cps[yh]

    for step, (block, there) in enumerate(blocks, 1):
        mine = m.ev.at[core, there]
        pltpu.make_async_remote_copy(
            mine, mine, m.g_send.at[step], m.g_recv.at[step], partner, MESH
        ).wait_recv()
        hand = pltpu.make_async_remote_copy(
            mine, mine, m.c_send.at[step], m.c_recv.at[step], partner, MESH
        )
        hand.start()
        sends.append(hand)

    arrived(m.cmr, *along_h, m.cm_send, m.cm_recv)
    m.bz0[z] = total(m.cmr, nyh)
    start(m.bz0, *along_z, m.z0_send, m.z_recv.at[0])

    def fill(step):
        block, there = blocks[step - 1]
        taken = m.ev.at[(core + 1) % nc, there]
        scales = m.rs.at[there]
        pltpu.make_async_remote_copy(
            scales, scales, m.r_send.at[step], m.r_recv.at[step], partner, MESH
        ).wait_recv()
        pltpu.make_async_remote_copy(
            taken, taken, m.c_send.at[step], m.c_recv.at[step], partner, MESH
        ).wait_recv()

        m.lg[step % 2] = dot_nt(block_rows(0, block), m.pr[yh])
        m.dot[aligned(block, per_block * LANES), :] = dot_nt(block_rows(1, block), m.pr[yh])
        for h in range(per_block):
            i = block * per_block + h
            rows = aligned(i)
            part_rows = slice(h * LANES, (h + 1) * LANES)
            scale = down(m.rs[i]) * mass_inverse
            for g, cols in enumerate(tiles_of(groups)):
                m.plan[rows, cols] = (
                    scale * m.cs[yh, g : g + 1, :] * jnp.exp2(m.lg[step % 2, part_rows, cols] * exp2_scale)
                )

    fill(1)
    arrived(m.cpr, *along_h, m.cp_send, m.cp_recv)
    m.bz[ITERS - 1, z] = total(m.cpr, nyh)
    start(m.bz.at[ITERS - 1], *along_z, m.z_send, m.z_recv.at[ITERS])
    for step in range(2, nyh):
        fill(step)
    finish(m.rsum, *along_h, m.q_send, m.q_recv)
    for block in range(nyh):
        place = slice(block * per_block, (block + 1) * per_block)
        m.row_mass[place, :] = m.rsum[block, :per_block, :]
        m.row_weight[place, :] = m.rsum[block, per_block:, :] * -view_scale
    for move in moves:
        move.wait()
    finish(m.bz0, *along_z, m.z0_send, m.z_recv.at[0])
    col_sums = total(m.bz0, nz)
    col_mass, col_weight = col_sums[0], col_sums[1] * -view_scale
    finish(m.bz.at[ITERS - 1], *along_z, m.z_send, m.z_recv.at[ITERS])
    col_dual = (col_weight - total(m.bz.at[ITERS - 1], nz)) / col_mass

    def column_part(row_dual, k):
        found = [jnp.zeros((8, LANES), F32)] * groups
        for i in range(chunks):
            dual = down(row_dual[i : i + 1, :])
            for g, cols in enumerate(tiles_of(groups)):
                found[g] = found[g] + fold(m.plan[i * LANES : (i + 1) * LANES, cols] * dual)
        for g in range(groups):
            m.bz[k, z, g : g + 1, :] = found[g].sum(0, keepdims=True)

    def row_part(col_dual, k):
        for i in range(chunks):
            rows = slice(i * LANES, (i + 1) * LANES)
            block = m.plan[rows, :LANES] * col_dual[0:1, :]
            for g, cols in enumerate(tiles_of(groups - 1, 1), 1):
                block = block + m.plan[rows, cols] * col_dual[g : g + 1, :]
            m.bx[k, xc, i : i + 1, :] = across(block)

    def sweep(k, duals):
        row_part(duals[1], k)
        start(m.bx.at[k], *along_x, m.x_send, m.x_recv.at[k])

        @pl.when(k == 0)
        def _():
            @pl.loop(0, chunks)
            def _(i):
                rows = aligned(i)
                m.splan[rows, :] = (m.plan[rows, :] * -view_scale).astype(BF16)

        finish(m.bx.at[k], *along_x, m.x_send, m.x_recv.at[k])
        m.by[k, y] = total(m.bx.at[k], nxc)
        start(m.by.at[k], *along_y, m.y_send, m.y_recv.at[k])

        @pl.when(k == 0)
        def _():
            @pl.loop(0, groups)
            def _(g):
                cols = aligned(g)
                m.tail[cols, :] = dot_tn(m.splan[:, cols], m.ev[1].reshape(chunks * LANES, width))

        finish(m.by.at[k], *along_y, m.y_send, m.y_recv.at[k])
        row_dual = (m.row_weight[...] - total(m.by.at[k], ny)) / m.row_mass[...]
        column_part(row_dual, k)
        start(m.bz.at[k], *along_z, m.z_send, m.z_recv.at[k + 1])
        finish(m.bz.at[k], *along_z, m.z_send, m.z_recv.at[k + 1])
        return row_dual, (col_weight - total(m.bz.at[k], nz)) / col_mass

    row_dual, col_dual = lax.fori_loop(
        0, ITERS - 1, sweep, (jnp.zeros((chunks, LANES), F32), col_dual)
    )

    m.bx[0, xc] = row_dual * (1.0 / view_scale)
    col_scaled = col_dual * (1.0 / view_scale)
    half = nx // per_block

    def last_chunk(block, h):
        i = block * per_block + h
        rows = aligned(i)
        dual = down(m.bx[0, xc, pl.ds(i, 1), :])
        for g, cols in enumerate(tiles_of(groups)):
            piece = m.plan[rows, cols] * (m.dot[rows, cols] + dual + col_scaled[g : g + 1, :])
            m.grad[rows, cols] = (-view_scale * logit_scale * piece).astype(BF16)
        product = jnp.dot(m.grad[rows, :], m.pr[yh], preferred_element_type=F32)
        m.eb[block, pl.ds(h * half, half)] = product.reshape(
            half, nyl, nc, LANES // (half * nyl * nc), width
        ).astype(BF16)

    for step in range(1, nyh + 1):
        block = (yh + step) % nyh

        for h in range(per_block):
            last_chunk(block, h)

        for turn in range(1, nxc):
            other = (xc + turn) % nxc
            sends.append(
                pltpu.make_async_remote_copy(
                    m.eb.at[block, other // nc, :, other % nc],
                    m.fx.at[block, xc],
                    m.fx_send.at[step - 1, turn],
                    m.fx_recv.at[block, xc],
                    at_xc(other),
                    MESH,
                )
            )
            sends[-1].start()

    for step in range(1, nz + 1):
        other = (z + step) % nz
        cols = aligned(other)
        share = m.tail[cols, :] + dot_tn(m.grad[:, cols], m.ev[0].reshape(chunks * LANES, width))
        if step < nz:
            m.pb[step] = share.astype(BF16)
            sends.append(
                pltpu.make_async_remote_copy(
                    m.pb.at[step], m.fz.at[z], m.fz_send.at[step], m.fz_recv.at[z], at_z(other), MESH
                )
            )
            sends[-1].start()
        else:
            pg_ref[...] = share

    for step in range(1, nyh + 1):
        block = (yh + step) % nyh
        arrived(m.fx.at[block], *along_x, m.fx_send.at[step - 1], m.fx_recv.at[block])
        part = m.eb[block, x, :, core].astype(F32)
        for turn in range(1, nxc):
            part = part + m.fx[block, (xc + turn) % nxc].astype(F32)
        m.fy_out[pl.ds(block * nyl, nyl)] = part
        for low in range(nyl):
            if step < nyh:
                other, slot = block * nyl + low, (step - 1) * nyl + low
            elif low:
                other, slot = yh * nyl + (yl + low) % nyl, (step - 1) * nyl + low
            else:
                continue
            sends.append(
                pltpu.make_async_remote_copy(
                    m.fy_out.at[other], m.fy.at[y], m.fy_send.at[slot], m.fy_recv.at[y], at_y(other), MESH
                )
            )
            sends[-1].start()

    arrived(m.fz, *along_z, m.fz_send, m.fz_recv)
    share = pg_ref[...]
    for step in range(1, nz):
        share = share + m.fz[(z + step) % nz].astype(F32)
    pg_ref[...] = share

    arrived(m.fy, *along_y, m.fy_send, m.fy_recv)
    rows_out = m.fy_out[y]
    for step in range(1, ny):
        rows_out = rows_out + m.fy[(y + step) % ny]
    eg_ref[...] = rows_out

    for send in sends:
        send.wait_send()


def build(mesh, dims):
    nx, nyl, nc, nyh, nz = dims
    ny, nxc, npr = nyl * nyh, nx * nc, nx * nyl * nc

    def per_device(embeddings, second_view, prototypes, row_scale, col_scale):
        row_count, width = embeddings.shape
        proto_count = prototypes.shape[0]
        proto_total = proto_count * npr
        rows, cols = row_count * nyh, proto_count // nyh
        per_block = row_count // LANES
        chunks, groups = rows // LANES, cols // LANES
        rows_out, cols_out = row_count // npr, cols // nz
        vmem, dma = pltpu.VMEM, pltpu.SemaphoreType.DMA
        scratch = dict(
            ev=vmem((2, chunks, LANES, width), BF16),
            pr=vmem((nyh, cols, width), BF16),
            rs=vmem((chunks, 1, LANES), F32),
            cs=vmem((nyh, groups, LANES), F32),
            plan0=vmem((nyh, row_count, cols), F32),
            dot0=vmem((nyh, row_count, cols), F32),
            plan=vmem((rows, cols), F32),
            dot=vmem((rows, cols), F32),
            lg=vmem((2, row_count, cols), F32),
            grad=vmem((rows, cols), BF16),
            splan=vmem((rows, cols), BF16),
            tail=vmem((cols, width), F32),
            colm=vmem((nyh, groups, 8, LANES), F32),
            colw=vmem((nyh, groups, 8, LANES), F32),
            rowm=vmem((per_block, LANES, LANES), F32),
            roww=vmem((per_block, LANES, LANES), F32),
            bw=vmem((npr, 2 * per_block, LANES), F32),
            rsum=vmem((nyh, 2 * per_block, LANES), F32),
            dual0=vmem((per_block, LANES), F32),
            row_mass=vmem((chunks, LANES), F32),
            row_weight=vmem((chunks, LANES), F32),
            cms=vmem((nyh, 2, groups, LANES), F32),
            cmr=vmem((nyh, 2, groups, LANES), F32),
            cps=vmem((nyh, groups, LANES), F32),
            cpr=vmem((nyh, groups, LANES), F32),
            bz0=vmem((nz, 2, groups, LANES), F32),
            bx=vmem((ITERS - 1, nxc, chunks, LANES), F32),
            by=vmem((ITERS - 1, ny, chunks, LANES), F32),
            bz=vmem((ITERS, nz, groups, LANES), F32),
            eb=vmem((nyh, nx, nyl, nc, rows_out, width), BF16),
            fx=vmem((nyh, nxc, nyl, rows_out, width), BF16),
            fy_out=vmem((ny, rows_out, width), F32),
            fy=vmem((ny, rows_out, width), F32),
            pb=vmem((nz, cols_out, width), BF16),
            fz=vmem((nz, cols_out, width), BF16),
            local_sem=dma((4,)),
            pro_sem=dma((nyh,)),
            g_send=dma((nyh,)),
            g_recv=dma((nyh,)),
            r_send=dma((nyh,)),
            r_recv=dma((nyh,)),
            c_send=dma((nyh,)),
            c_recv=dma((nyh,)),
            w_send=dma((npr,)),
            w_recv=dma((npr,)),
            q_send=dma((nyh,)),
            q_recv=dma((nyh,)),
            cm_send=dma((nyh,)),
            cm_recv=dma((nyh,)),
            cp_send=dma((nyh,)),
            cp_recv=dma((nyh,)),
            x_send=dma((nxc,)),
            y_send=dma((ny,)),
            z_send=dma((nz,)),
            z0_send=dma((nz,)),
            x_recv=dma((ITERS - 1, nxc)),
            y_recv=dma((ITERS - 1, ny)),
            z_recv=dma((ITERS + 1, nz)),
            fx_send=dma((nyh, nxc)),
            fx_recv=dma((nyh, nxc)),
            fy_send=dma((ny,)),
            fy_recv=dma((ny,)),
            fz_send=dma((nz,)),
            fz_recv=dma((nz,)),
        )
        return pl.pallas_call(
            functools.partial(kernel, dims, proto_total, tuple(scratch)),
            out_shape=(
                jax.ShapeDtypeStruct((rows_out, width), F32),
                jax.ShapeDtypeStruct((cols_out, width), F32),
            ),
            in_specs=[pl.BlockSpec(memory_space=pltpu.HBM)] * 5,
            out_specs=(pl.BlockSpec(memory_space=pltpu.VMEM),) * 2,
            scratch_shapes=list(scratch.values()),
            compiler_params=pltpu.CompilerParams(
                collective_id=0, has_side_effects=True, vmem_limit_bytes=40 * 1024 * 1024
            ),
        )(
            *[
                pltpu.with_memory_space_constraint(array, pltpu.HBM)
                for array in (
                    embeddings.reshape(per_block, LANES, width),
                    second_view.reshape(per_block, LANES, width),
                    prototypes.reshape(nyh, cols, width),
                    row_scale.reshape(per_block, 1, LANES),
                    col_scale.reshape(nyh, groups, LANES),
                )
            ]
        )

    return jax.shard_map(
        per_device,
        mesh=mesh,
        in_specs=(P("row", None), P("row", None), P("proto", None), P("row"), P("proto")),
        out_specs=(P(("row", "proto"), None), P(("proto", "row"), None)),
        check_vma=False,
    )


def solution(mesh):
    return build(mesh, DIMS)
```

```python
import functools
import math
from types import SimpleNamespace

import jax
import jax.numpy as jnp
from jax import lax
from jax.experimental import pallas as pl
from jax.experimental.pallas import tpu as pltpu
from jax.sharding import PartitionSpec as P

ITERS = 4
LANES = 128
MESH = pl.DeviceIdType.MESH
F32 = jnp.float32
BF16 = jnp.bfloat16

DIMS = (4, 2, 2, 4, 8)


def dot_nt(left, right):
    return lax.dot_general(left, right, (((1,), (1,)), ((), ())), preferred_element_type=F32)


def dot_tn(left, right):
    return lax.dot_general(left, right, (((0,), (0,)), ((), ())), preferred_element_type=F32)


def down(row):
    return jnp.broadcast_to(row, (LANES, LANES)).T


def fold(block):
    return block.reshape(block.shape[0] // 8, 8, LANES).sum(0)


def across(block):
    return block.T.sum(0, keepdims=True)


def tiles_of(count, start=0):
    return [slice((start + g) * LANES, (start + g + 1) * LANES) for g in range(count)]


def aligned(i, size=LANES):
    return pl.ds(pl.multiple_of(i * size, size), size)


def far_first(count):
    return sorted(range(1, count), key=lambda step: -min(step, count - step))


def kernel(dims, proto_total, names, emb_in, view_in, pro_in, rs_in, cs_in, eg_ref, pg_ref, *scratch):
    m = SimpleNamespace(**dict(zip(names, scratch)))
    nx, nyl, nc, nyh, nz = dims
    ny, nxc, npr = nyl * nyh, nx * nc, nx * nyl * nc
    row_id, me_p = lax.axis_index("row"), lax.axis_index("proto")
    yh, z = row_id // nz, row_id % nz
    core = me_p % nc
    yl = (me_p // nc) % nyl
    x = me_p // (nc * nyl)
    y = yh * nyl + yl
    xc = x * nc + core

    def at_z(other):
        return (yh * nz + other, me_p)

    def at_yh(other):
        return (other * nz + z, me_p)

    def at_y(other):
        return ((other // nyl) * nz + z, (x * nyl + other % nyl) * nc + core)

    def at_xc(other):
        return (row_id, ((other // nc) * nyl + yl) * nc + other % nc)

    def at_p(other):
        return (row_id, other)

    chunks, groups = m.plan.shape[0] // LANES, m.plan.shape[1] // LANES
    per_block = chunks // nyh
    width = emb_in.shape[-1]
    logit_scale = 1.0 / (0.05 * width)
    view_scale = 1.0 / (0.1 * width)
    mass_inverse = 1.0 / (64.0 * proto_total)
    exp2_scale = logit_scale * math.log2(math.e)

    own = pl.ds(yh * per_block, per_block)
    small_loads = [
        pltpu.make_async_copy(emb_in, m.ev.at[0, own], m.local_sem.at[0]),
        pltpu.make_async_copy(view_in, m.ev.at[1, own], m.local_sem.at[1]),
        pltpu.make_async_copy(rs_in, m.rs.at[own], m.local_sem.at[2]),
        pltpu.make_async_copy(cs_in, m.cs, m.local_sem.at[3]),
    ]
    for load in small_loads:
        load.start()

    def pro_load(part):
        return pltpu.make_async_copy(pro_in.at[part], m.pr.at[part], m.pro_sem.at[part])

    for part in range(nyh):
        pro_load(part).start()

    barrier = pltpu.get_barrier_semaphore()
    for count, me, address in ((nz, z, at_z), (ny, y, at_y), (npr, me_p, at_p)):
        for step in range(1, count):
            pl.semaphore_signal(
                barrier, inc=1, device_id=address((me + step) % count), device_id_type=MESH
            )
    for load in small_loads:
        load.wait()

    m.rowm[...] = jnp.zeros_like(m.rowm)
    m.roww[...] = jnp.zeros_like(m.roww)

    def own_part(part):
        for h in range(per_block):
            rows = slice(h * LANES, (h + 1) * LANES)
            scale = down(m.rs[yh * per_block + h]) * mass_inverse
            mass = m.rowm[h]
            weight = m.roww[h]
            for g, cols in enumerate(tiles_of(groups)):
                value = scale * m.cs[part, g : g + 1, :] * jnp.exp2(m.lg[part % 2, rows, cols] * exp2_scale)
                m.plan0[part, rows, cols] = value
                weighted = value * m.dot0[part, rows, cols]
                mass = mass + value
                weight = weight + weighted
                if h:
                    m.colm[part, g] += fold(value)
                    m.colw[part, g] += fold(weighted)
                else:
                    m.colm[part, g] = fold(value)
                    m.colw[part, g] = fold(weighted)
            m.rowm[h] = mass
            m.roww[h] = weight

    def block_rows(kind, block):
        place = pl.ds(block * per_block, per_block)
        return m.ev[kind, place].reshape(per_block * LANES, width)

    def own_parts(first, last):
        for part in range(first, last):
            pro_load(part).wait()
        for part in range(first, last):
            m.lg[part % 2] = dot_nt(block_rows(0, yh), m.pr[part])
            m.dot0[part] = dot_nt(block_rows(1, yh), m.pr[part])
            own_part(part)

    own_parts(0, nyh // 2)
    own_parts(nyh // 2, nyh)
    sends = []

    def start(slots, me, count, address, send, recv):
        for step in far_first(count):
            other = (me + step) % count
            pltpu.make_async_remote_copy(
                slots.at[me], slots.at[me], send.at[step], recv.at[me], address(other), MESH
            ).start()

    def finish(slots, me, count, address, send, recv):
        for step in range(1, count):
            other = (me + step) % count
            pltpu.make_async_remote_copy(
                slots.at[other], slots.at[other], send.at[step], recv.at[other], address(other), MESH
            ).wait_recv()
        for step in range(1, count):
            other = (me + step) % count
            pltpu.make_async_remote_copy(
                slots.at[me], slots.at[me], send.at[step], recv.at[me], address(other), MESH
            ).wait_send()

    def scatter(shares, slots, me, count, address, send, recv):
        copies = []
        for step in far_first(count):
            other = (me + step) % count
            copies.append(
                pltpu.make_async_remote_copy(
                    shares.at[other], slots.at[me], send.at[step], recv.at[me], address(other), MESH
                )
            )
            copies[-1].start()
        return copies

    def arrived(slots, me, count, address, send, recv):
        for step in range(1, count):
            other = (me + step) % count
            pltpu.make_async_remote_copy(
                slots.at[other], slots.at[other], send.at[step], recv.at[other], address(other), MESH
            ).wait_recv()

    def total(slots, count):
        result = slots[0]
        for slot in range(1, count):
            result = result + slots[slot]
        return result

    along_x = (xc, nxc, at_xc)
    along_y = (y, ny, at_y)
    along_z = (z, nz, at_z)
    along_p = (me_p, npr, at_p)
    along_h = (yh, nyh, at_yh)

    for h in range(per_block):
        m.bw[me_p, h : h + 1, :] = across(m.rowm[h])
        m.bw[me_p, per_block + h : per_block + h + 1, :] = across(m.roww[h])
    pl.semaphore_wait(barrier, nz + ny + npr - 3)
    start(m.bw, *along_p, m.w_send, m.w_recv)

    sign = 2 * yl - 1
    partner = at_xc(x * nc + (core + 1) % nc)
    blocks = []
    for step in range(1, nyh):
        target = (y + sign * step + ny) % ny
        source = (y + (sign if step % 2 else -sign) * step + ny) % ny
        blocks.append((source // nyl, pl.ds((source // nyl) * per_block, per_block)))
        rows_out = pltpu.make_async_remote_copy(
            m.ev.at[core, own], m.ev.at[core, own], m.g_send.at[step], m.g_recv.at[step], at_y(target), MESH
        )
        scale_out = pltpu.make_async_remote_copy(
            m.rs.at[own], m.rs.at[own], m.r_send.at[step], m.r_recv.at[step], at_y(target), MESH
        )
        rows_out.start()
        scale_out.start()
        sends += [rows_out, scale_out]

    own_rows = aligned(yh, per_block * LANES)
    moves = [
        pltpu.make_async_copy(m.plan0.at[yh], m.plan.at[own_rows], m.local_sem.at[0]),
        pltpu.make_async_copy(m.dot0.at[yh], m.dot.at[own_rows], m.local_sem.at[1]),
    ]
    for move in moves:
        move.start()

    for part in range(nyh):
        for g in range(groups):
            m.cms[part, 0, g : g + 1, :] = m.colm[part, g].sum(0, keepdims=True)
            m.cms[part, 1, g : g + 1, :] = m.colw[part, g].sum(0, keepdims=True)
    sends += scatter(m.cms, m.cmr, *along_h, m.cm_send, m.cm_recv)
    m.cmr[yh] = m.cms[yh]

    finish(m.bw, *along_p, m.w_send, m.w_recv)
    sums = total(m.bw, npr)
    m.rsum[yh] = sums
    m.dual0[...] = sums[per_block:] * -view_scale / sums[:per_block]
    start(m.rsum, *along_h, m.q_send, m.q_recv)

    for part in range(nyh):
        found = [jnp.zeros((8, LANES), F32)] * groups
        for h in range(per_block):
            dual = down(m.dual0[h : h + 1, :])
            for g, cols in enumerate(tiles_of(groups)):
                found[g] = found[g] + fold(m.plan0[part, h * LANES : (h + 1) * LANES, cols] * dual)
        for g in range(groups):
            m.cps[part, g : g + 1, :] = found[g].sum(0, keepdims=True)

    sends += scatter(m.cps, m.cpr, *along_h, m.cp_send, m.cp_recv)
    m.cpr[yh] = m.cps[yh]

    for step, (block, there) in enumerate(blocks, 1):
        mine = m.ev.at[core, there]
        pltpu.make_async_remote_copy(
            mine, mine, m.g_send.at[step], m.g_recv.at[step], partner, MESH
        ).wait_recv()
        hand = pltpu.make_async_remote_copy(
            mine, mine, m.c_send.at[step], m.c_recv.at[step], partner, MESH
        )
        hand.start()
        sends.append(hand)

    arrived(m.cmr, *along_h, m.cm_send, m.cm_recv)
    m.bz0[z] = total(m.cmr, nyh)
    start(m.bz0, *along_z, m.z0_send, m.z_recv.at[0])

    def fill(step):
        block, there = blocks[step - 1]
        taken = m.ev.at[(core + 1) % nc, there]
        scales = m.rs.at[there]
        pltpu.make_async_remote_copy(
            scales, scales, m.r_send.at[step], m.r_recv.at[step], partner, MESH
        ).wait_recv()
        pltpu.make_async_remote_copy(
            taken, taken, m.c_send.at[step], m.c_recv.at[step], partner, MESH
        ).wait_recv()

        m.lg[step % 2] = dot_nt(block_rows(0, block), m.pr[yh])
        m.dot[aligned(block, per_block * LANES), :] = dot_nt(block_rows(1, block), m.pr[yh])
        for h in range(per_block):
            i = block * per_block + h
            rows = aligned(i)
            part_rows = slice(h * LANES, (h + 1) * LANES)
            scale = down(m.rs[i]) * mass_inverse
            for g, cols in enumerate(tiles_of(groups)):
                m.plan[rows, cols] = (
                    scale * m.cs[yh, g : g + 1, :] * jnp.exp2(m.lg[step % 2, part_rows, cols] * exp2_scale)
                )

    arrived(m.cpr, *along_h, m.cp_send, m.cp_recv)
    m.bz[ITERS - 1, z] = total(m.cpr, nyh)
    start(m.bz.at[ITERS - 1], *along_z, m.z_send, m.z_recv.at[ITERS])
    for step in range(1, nyh):
        fill(step)
    finish(m.rsum, *along_h, m.q_send, m.q_recv)
    for block in range(nyh):
        place = slice(block * per_block, (block + 1) * per_block)
        m.row_mass[place, :] = m.rsum[block, :per_block, :]
        m.row_weight[place, :] = m.rsum[block, per_block:, :] * -view_scale
    for move in moves:
        move.wait()
    finish(m.bz0, *along_z, m.z0_send, m.z_recv.at[0])
    col_sums = total(m.bz0, nz)
    col_mass, col_weight = col_sums[0], col_sums[1] * -view_scale
    finish(m.bz.at[ITERS - 1], *along_z, m.z_send, m.z_recv.at[ITERS])
    col_dual = (col_weight - total(m.bz.at[ITERS - 1], nz)) / col_mass

    def column_part(row_dual, k):
        found = [jnp.zeros((8, LANES), F32)] * groups
        for i in range(chunks):
            dual = down(row_dual[i : i + 1, :])
            for g, cols in enumerate(tiles_of(groups)):
                found[g] = found[g] + fold(m.plan[i * LANES : (i + 1) * LANES, cols] * dual)
        for g in range(groups):
            m.bz[k, z, g : g + 1, :] = found[g].sum(0, keepdims=True)

    def row_part(col_dual, k):
        for i in range(chunks):
            rows = slice(i * LANES, (i + 1) * LANES)
            block = m.plan[rows, :LANES] * col_dual[0:1, :]
            for g, cols in enumerate(tiles_of(groups - 1, 1), 1):
                block = block + m.plan[rows, cols] * col_dual[g : g + 1, :]
            m.bx[k, xc, i : i + 1, :] = across(block)

    def sweep(k, duals):
        row_part(duals[1], k)
        start(m.bx.at[k], *along_x, m.x_send, m.x_recv.at[k])

        @pl.when(k == 0)
        def _():
            @pl.loop(0, chunks)
            def _(i):
                rows = aligned(i)
                m.splan[rows, :] = (m.plan[rows, :] * -view_scale).astype(BF16)

        finish(m.bx.at[k], *along_x, m.x_send, m.x_recv.at[k])
        m.by[k, y] = total(m.bx.at[k], nxc)
        start(m.by.at[k], *along_y, m.y_send, m.y_recv.at[k])

        @pl.when(k == 0)
        def _():
            @pl.loop(0, groups)
            def _(g):
                cols = aligned(g)
                m.tail[cols, :] = dot_tn(m.splan[:, cols], m.ev[1].reshape(chunks * LANES, width))

        finish(m.by.at[k], *along_y, m.y_send, m.y_recv.at[k])
        row_dual = (m.row_weight[...] - total(m.by.at[k], ny)) / m.row_mass[...]
        column_part(row_dual, k)
        start(m.bz.at[k], *along_z, m.z_send, m.z_recv.at[k + 1])
        finish(m.bz.at[k], *along_z, m.z_send, m.z_recv.at[k + 1])
        return row_dual, (col_weight - total(m.bz.at[k], nz)) / col_mass

    row_dual, col_dual = lax.fori_loop(
        0, ITERS - 1, sweep, (jnp.zeros((chunks, LANES), F32), col_dual)
    )

    m.bx[0, xc] = row_dual * (1.0 / view_scale)
    col_scaled = col_dual * (1.0 / view_scale)
    half = nx // per_block

    def last_chunk(block, h):
        i = block * per_block + h
        rows = aligned(i)
        dual = down(m.bx[0, xc, pl.ds(i, 1), :])
        for g, cols in enumerate(tiles_of(groups)):
            piece = m.plan[rows, cols] * (m.dot[rows, cols] + dual + col_scaled[g : g + 1, :])
            m.grad[rows, cols] = (-view_scale * logit_scale * piece).astype(BF16)
        product = jnp.dot(m.grad[rows, :], m.pr[yh], preferred_element_type=F32)
        m.eb[block, pl.ds(h * half, half)] = product.reshape(
            half, nyl, nc, LANES // (half * nyl * nc), width
        ).astype(BF16)

    for step in range(1, nyh + 1):
        block = (yh + step) % nyh

        for h in range(per_block):
            last_chunk(block, h)

        for turn in range(1, nxc):
            other = (xc + turn) % nxc
            sends.append(
                pltpu.make_async_remote_copy(
                    m.eb.at[block, other // nc, :, other % nc],
                    m.fx.at[block, xc],
                    m.fx_send.at[step - 1, turn],
                    m.fx_recv.at[block, xc],
                    at_xc(other),
                    MESH,
                )
            )
            sends[-1].start()
        if step < nyh:
            m.tail[...] += dot_tn(m.grad[aligned(block, per_block * LANES), :], block_rows(0, block))

    for step in far_first(nz) + [nz]:
        other = (z + step) % nz
        cols = aligned(other)
        share = m.tail[cols, :] + dot_tn(m.grad[own_rows, cols], block_rows(0, yh))
        if step < nz:
            m.pb[step] = share.astype(BF16)
            sends.append(
                pltpu.make_async_remote_copy(
                    m.pb.at[step], m.fz.at[z], m.fz_send.at[step], m.fz_recv.at[z], at_z(other), MESH
                )
            )
            sends[-1].start()
        else:
            pg_ref[...] = share

    for step in range(1, nyh + 1):
        block = (yh + step) % nyh
        arrived(m.fx.at[block], *along_x, m.fx_send.at[step - 1], m.fx_recv.at[block])
        part = m.eb[block, x, :, core].astype(F32)
        for turn in range(1, nxc):
            part = part + m.fx[block, (xc + turn) % nxc].astype(F32)
        m.fy_out[pl.ds(block * nyl, nyl)] = part
        for low in range(nyl):
            if step < nyh:
                other, slot = block * nyl + low, (step - 1) * nyl + low
            elif low:
                other, slot = yh * nyl + (yl + low) % nyl, (step - 1) * nyl + low
            else:
                continue
            sends.append(
                pltpu.make_async_remote_copy(
                    m.fy_out.at[other], m.fy.at[y], m.fy_send.at[slot], m.fy_recv.at[y], at_y(other), MESH
                )
            )
            sends[-1].start()

    arrived(m.fz, *along_z, m.fz_send, m.fz_recv)
    share = pg_ref[...]
    for step in range(1, nz):
        share = share + m.fz[(z + step) % nz].astype(F32)
    pg_ref[...] = share

    arrived(m.fy, *along_y, m.fy_send, m.fy_recv)
    rows_out = m.fy_out[y]
    for step in range(1, ny):
        rows_out = rows_out + m.fy[(y + step) % ny]
    eg_ref[...] = rows_out

    for send in sends:
        send.wait_send()


def build(mesh, dims):
    nx, nyl, nc, nyh, nz = dims
    ny, nxc, npr = nyl * nyh, nx * nc, nx * nyl * nc

    def per_device(embeddings, second_view, prototypes, row_scale, col_scale):
        row_count, width = embeddings.shape
        proto_count = prototypes.shape[0]
        proto_total = proto_count * npr
        rows, cols = row_count * nyh, proto_count // nyh
        per_block = row_count // LANES
        chunks, groups = rows // LANES, cols // LANES
        rows_out, cols_out = row_count // npr, cols // nz
        vmem, dma = pltpu.VMEM, pltpu.SemaphoreType.DMA
        scratch = dict(
            ev=vmem((2, chunks, LANES, width), BF16),
            pr=vmem((nyh, cols, width), BF16),
            rs=vmem((chunks, 1, LANES), F32),
            cs=vmem((nyh, groups, LANES), F32),
            plan0=vmem((nyh, row_count, cols), F32),
            dot0=vmem((nyh, row_count, cols), F32),
            plan=vmem((rows, cols), F32),
            dot=vmem((rows, cols), F32),
            lg=vmem((2, row_count, cols), F32),
            grad=vmem((rows, cols), BF16),
            splan=vmem((rows, cols), BF16),
            tail=vmem((cols, width), F32),
            colm=vmem((nyh, groups, 8, LANES), F32),
            colw=vmem((nyh, groups, 8, LANES), F32),
            rowm=vmem((per_block, LANES, LANES), F32),
            roww=vmem((per_block, LANES, LANES), F32),
            bw=vmem((npr, 2 * per_block, LANES), F32),
            rsum=vmem((nyh, 2 * per_block, LANES), F32),
            dual0=vmem((per_block, LANES), F32),
            row_mass=vmem((chunks, LANES), F32),
            row_weight=vmem((chunks, LANES), F32),
            cms=vmem((nyh, 2, groups, LANES), F32),
            cmr=vmem((nyh, 2, groups, LANES), F32),
            cps=vmem((nyh, groups, LANES), F32),
            cpr=vmem((nyh, groups, LANES), F32),
            bz0=vmem((nz, 2, groups, LANES), F32),
            bx=vmem((ITERS - 1, nxc, chunks, LANES), F32),
            by=vmem((ITERS - 1, ny, chunks, LANES), F32),
            bz=vmem((ITERS, nz, groups, LANES), F32),
            eb=vmem((nyh, nx, nyl, nc, rows_out, width), BF16),
            fx=vmem((nyh, nxc, nyl, rows_out, width), BF16),
            fy_out=vmem((ny, rows_out, width), F32),
            fy=vmem((ny, rows_out, width), F32),
            pb=vmem((nz, cols_out, width), BF16),
            fz=vmem((nz, cols_out, width), BF16),
            local_sem=dma((4,)),
            pro_sem=dma((nyh,)),
            g_send=dma((nyh,)),
            g_recv=dma((nyh,)),
            r_send=dma((nyh,)),
            r_recv=dma((nyh,)),
            c_send=dma((nyh,)),
            c_recv=dma((nyh,)),
            w_send=dma((npr,)),
            w_recv=dma((npr,)),
            q_send=dma((nyh,)),
            q_recv=dma((nyh,)),
            cm_send=dma((nyh,)),
            cm_recv=dma((nyh,)),
            cp_send=dma((nyh,)),
            cp_recv=dma((nyh,)),
            x_send=dma((nxc,)),
            y_send=dma((ny,)),
            z_send=dma((nz,)),
            z0_send=dma((nz,)),
            x_recv=dma((ITERS - 1, nxc)),
            y_recv=dma((ITERS - 1, ny)),
            z_recv=dma((ITERS + 1, nz)),
            fx_send=dma((nyh, nxc)),
            fx_recv=dma((nyh, nxc)),
            fy_send=dma((ny,)),
            fy_recv=dma((ny,)),
            fz_send=dma((nz,)),
            fz_recv=dma((nz,)),
        )
        return pl.pallas_call(
            functools.partial(kernel, dims, proto_total, tuple(scratch)),
            out_shape=(
                jax.ShapeDtypeStruct((rows_out, width), F32),
                jax.ShapeDtypeStruct((cols_out, width), F32),
            ),
            in_specs=[pl.BlockSpec(memory_space=pltpu.HBM)] * 5,
            out_specs=(pl.BlockSpec(memory_space=pltpu.VMEM),) * 2,
            scratch_shapes=list(scratch.values()),
            compiler_params=pltpu.CompilerParams(
                collective_id=0, has_side_effects=True, vmem_limit_bytes=40 * 1024 * 1024
            ),
        )(
            *[
                pltpu.with_memory_space_constraint(array, pltpu.HBM)
                for array in (
                    embeddings.reshape(per_block, LANES, width),
                    second_view.reshape(per_block, LANES, width),
                    prototypes.reshape(nyh, cols, width),
                    row_scale.reshape(per_block, 1, LANES),
                    col_scale.reshape(nyh, groups, LANES),
                )
            ]
        )

    return jax.shard_map(
        per_device,
        mesh=mesh,
        in_specs=(P("row", None), P("row", None), P("proto", None), P("row"), P("proto")),
        out_specs=(P(("row", "proto"), None), P(("proto", "row"), None)),
        check_vma=False,
    )


def solution(mesh):
    return build(mesh, DIMS)
```

```python
import functools
import math
from types import SimpleNamespace

import jax
import jax.numpy as jnp
from jax import lax
from jax.experimental import pallas as pl
from jax.experimental.pallas import tpu as pltpu
from jax.sharding import PartitionSpec as P

ITERS = 4
LANES = 128
MESH = pl.DeviceIdType.MESH
F32 = jnp.float32
BF16 = jnp.bfloat16

DIMS = (4, 2, 2, 4, 8)


def dot_nt(left, right):
    return lax.dot_general(left, right, (((1,), (1,)), ((), ())), preferred_element_type=F32)


def dot_tn(left, right):
    return lax.dot_general(left, right, (((0,), (0,)), ((), ())), preferred_element_type=F32)


def down(row):
    return jnp.broadcast_to(row, (LANES, LANES)).T


def fold(block):
    return block.reshape(block.shape[0] // 8, 8, LANES).sum(0)


def across(block):
    return block.T.sum(0, keepdims=True)


def tiles_of(count, start=0):
    return [slice((start + g) * LANES, (start + g + 1) * LANES) for g in range(count)]


def aligned(i, size=LANES):
    return pl.ds(pl.multiple_of(i * size, size), size)


def far_first(count):
    return sorted(range(1, count), key=lambda step: -min(step, count - step))


def kernel(dims, proto_total, names, emb_in, view_in, pro_in, rs_in, cs_in, eg_ref, pg_ref, *scratch):
    m = SimpleNamespace(**dict(zip(names, scratch)))
    nx, nyl, nc, nyh, nz = dims
    ny, nxc, npr = nyl * nyh, nx * nc, nx * nyl * nc
    row_id, me_p = lax.axis_index("row"), lax.axis_index("proto")
    yh, z = row_id // nz, row_id % nz
    core = me_p % nc
    yl = (me_p // nc) % nyl
    x = me_p // (nc * nyl)
    y = yh * nyl + yl
    xc = x * nc + core

    def at_z(other):
        return (yh * nz + other, me_p)

    def at_yh(other):
        return (other * nz + z, me_p)

    def at_y(other):
        return ((other // nyl) * nz + z, (x * nyl + other % nyl) * nc + core)

    def at_xc(other):
        return (row_id, ((other // nc) * nyl + yl) * nc + other % nc)

    def at_p(other):
        return (row_id, other)

    chunks, groups = m.plan.shape[0] // LANES, m.plan.shape[1] // LANES
    per_block = chunks // nyh
    width = emb_in.shape[-1]
    logit_scale = 1.0 / (0.05 * width)
    view_scale = 1.0 / (0.1 * width)
    mass_inverse = 1.0 / (64.0 * proto_total)
    view_shift = 2.0 ** math.ceil(-math.log2(view_scale))
    cot_scale = -view_scale * view_shift
    exp2_scale = logit_scale * math.log2(math.e)

    own = pl.ds(yh * per_block, per_block)
    small_loads = [
        pltpu.make_async_copy(emb_in, m.ev.at[0, own], m.local_sem.at[0]),
        pltpu.make_async_copy(view_in, m.ev.at[1, own], m.local_sem.at[1]),
        pltpu.make_async_copy(rs_in, m.rs.at[own], m.local_sem.at[2]),
        pltpu.make_async_copy(cs_in, m.cs, m.local_sem.at[3]),
    ]
    for load in small_loads:
        load.start()

    def pro_load(part):
        return pltpu.make_async_copy(pro_in.at[part], m.pr.at[part], m.pro_sem.at[part])

    for part in range(nyh):
        pro_load(part).start()

    barrier = pltpu.get_barrier_semaphore()
    for count, me, address in ((nz, z, at_z), (ny, y, at_y), (npr, me_p, at_p)):
        for step in range(1, count):
            pl.semaphore_signal(
                barrier, inc=1, device_id=address((me + step) % count), device_id_type=MESH
            )
    for load in small_loads:
        load.wait()
    m.ev[1, own] = (m.ev[1, own].astype(F32) * (1.0 / view_shift)).astype(BF16)

    m.rowm[...] = jnp.zeros_like(m.rowm)
    m.roww[...] = jnp.zeros_like(m.roww)

    def own_part(part):
        for h in range(per_block):
            rows = slice(h * LANES, (h + 1) * LANES)
            scale = down(m.rs[yh * per_block + h]) * mass_inverse
            mass = m.rowm[h]
            weight = m.roww[h]
            for g, cols in enumerate(tiles_of(groups)):
                value = scale * m.cs[part, g : g + 1, :] * jnp.exp2(m.lg[part % 2, rows, cols] * exp2_scale)
                m.plan0[part, rows, cols] = value
                weighted = value * m.dot0[part, rows, cols]
                mass = mass + value
                weight = weight + weighted
            m.rowm[h] = mass
            m.roww[h] = weight

    def block_rows(kind, block):
        place = pl.ds(block * per_block, per_block)
        return m.ev[kind, place].reshape(per_block * LANES, width)

    def own_parts(first, last):
        for part in range(first, last):
            pro_load(part).wait()
        for part in range(first, last):
            m.lg[part % 2] = dot_nt(block_rows(0, yh), m.pr[part])
            m.dot0[part] = dot_nt(block_rows(1, yh), m.pr[part])
            own_part(part)

    own_parts(0, nyh // 2)
    own_parts(nyh // 2, nyh)
    sends = []

    def start(slots, me, count, address, send, recv):
        for step in far_first(count):
            other = (me + step) % count
            pltpu.make_async_remote_copy(
                slots.at[me], slots.at[me], send.at[step], recv.at[me], address(other), MESH
            ).start()

    def finish(slots, me, count, address, send, recv):
        for step in range(1, count):
            other = (me + step) % count
            pltpu.make_async_remote_copy(
                slots.at[other], slots.at[other], send.at[step], recv.at[other], address(other), MESH
            ).wait_recv()
        for step in range(1, count):
            other = (me + step) % count
            pltpu.make_async_remote_copy(
                slots.at[me], slots.at[me], send.at[step], recv.at[me], address(other), MESH
            ).wait_send()

    def scatter(shares, slots, me, count, address, send, recv):
        copies = []
        for step in far_first(count):
            other = (me + step) % count
            copies.append(
                pltpu.make_async_remote_copy(
                    shares.at[other], slots.at[me], send.at[step], recv.at[me], address(other), MESH
                )
            )
            copies[-1].start()
        return copies

    def arrived(slots, me, count, address, send, recv):
        for step in range(1, count):
            other = (me + step) % count
            pltpu.make_async_remote_copy(
                slots.at[other], slots.at[other], send.at[step], recv.at[other], address(other), MESH
            ).wait_recv()

    def total(slots, count):
        result = slots[0]
        for slot in range(1, count):
            result = result + slots[slot]
        return result

    along_x = (xc, nxc, at_xc)
    along_y = (y, ny, at_y)
    along_z = (z, nz, at_z)
    along_p = (me_p, npr, at_p)
    along_h = (yh, nyh, at_yh)

    for h in range(per_block):
        m.bw[me_p, h : h + 1, :] = across(m.rowm[h])
        m.bw[me_p, per_block + h : per_block + h + 1, :] = across(m.roww[h])
    pl.semaphore_wait(barrier, nz + ny + npr - 3)
    start(m.bw, *along_p, m.w_send, m.w_recv)

    sign = 2 * yl - 1
    partner = at_xc(x * nc + (core + 1) % nc)
    blocks = []
    for step in range(1, nyh):
        target = (y + sign * step + ny) % ny
        source = (y + (sign if step % 2 else -sign) * step + ny) % ny
        blocks.append((source // nyl, pl.ds((source // nyl) * per_block, per_block)))
        rows_out = pltpu.make_async_remote_copy(
            m.ev.at[core, own], m.ev.at[core, own], m.g_send.at[step], m.g_recv.at[step], at_y(target), MESH
        )
        scale_out = pltpu.make_async_remote_copy(
            m.rs.at[own], m.rs.at[own], m.r_send.at[step], m.r_recv.at[step], at_y(target), MESH
        )
        rows_out.start()
        scale_out.start()
        sends += [rows_out, scale_out]

    own_rows = aligned(yh, per_block * LANES)
    moves = [
        pltpu.make_async_copy(m.plan0.at[yh], m.plan.at[own_rows], m.local_sem.at[0]),
        pltpu.make_async_copy(m.dot0.at[yh], m.dot.at[own_rows], m.local_sem.at[1]),
    ]
    for move in moves:
        move.start()

    @pl.loop(0, nyh)
    def _(part):
        for g, cols in enumerate(tiles_of(groups)):
            value = m.plan0[part, :, cols]
            m.cms[part, 0, g : g + 1, :] = fold(value).sum(0, keepdims=True)
            value = value * m.dot0[part, :, cols]
            m.cms[part, 1, g : g + 1, :] = fold(value).sum(0, keepdims=True)

    sends += scatter(m.cms, m.cmr, *along_h, m.cm_send, m.cm_recv)
    m.cmr[yh] = m.cms[yh]

    finish(m.bw, *along_p, m.w_send, m.w_recv)
    sums = total(m.bw, npr)
    m.rsum[yh] = sums
    m.dual0[...] = sums[per_block:] * cot_scale / sums[:per_block]
    start(m.rsum, *along_h, m.q_send, m.q_recv)

    for part in range(nyh):
        found = [jnp.zeros((8, LANES), F32)] * groups
        for h in range(per_block):
            dual = down(m.dual0[h : h + 1, :])
            for g, cols in enumerate(tiles_of(groups)):
                found[g] = found[g] + fold(m.plan0[part, h * LANES : (h + 1) * LANES, cols] * dual)
        for g in range(groups):
            m.cps[part, g : g + 1, :] = found[g].sum(0, keepdims=True)

    sends += scatter(m.cps, m.cpr, *along_h, m.cp_send, m.cp_recv)
    m.cpr[yh] = m.cps[yh]

    for step, (block, there) in enumerate(blocks, 1):
        mine = m.ev.at[core, there]
        pltpu.make_async_remote_copy(
            mine, mine, m.g_send.at[step], m.g_recv.at[step], partner, MESH
        ).wait_recv()
        hand = pltpu.make_async_remote_copy(
            mine, mine, m.c_send.at[step], m.c_recv.at[step], partner, MESH
        )
        hand.start()
        sends.append(hand)

    arrived(m.cmr, *along_h, m.cm_send, m.cm_recv)
    m.bz0[z] = total(m.cmr, nyh)
    start(m.bz0, *along_z, m.z0_send, m.z_recv.at[0])

    def fill(step):
        block, there = blocks[step - 1]
        taken = m.ev.at[(core + 1) % nc, there]
        scales = m.rs.at[there]
        pltpu.make_async_remote_copy(
            scales, scales, m.r_send.at[step], m.r_recv.at[step], partner, MESH
        ).wait_recv()
        pltpu.make_async_remote_copy(
            taken, taken, m.c_send.at[step], m.c_recv.at[step], partner, MESH
        ).wait_recv()

        m.lg[step % 2] = dot_nt(block_rows(0, block), m.pr[yh])
        m.dot[aligned(block, per_block * LANES), :] = dot_nt(block_rows(1, block), m.pr[yh])
        for h in range(per_block):
            i = block * per_block + h
            rows = aligned(i)
            part_rows = slice(h * LANES, (h + 1) * LANES)
            scale = down(m.rs[i]) * mass_inverse
            for g, cols in enumerate(tiles_of(groups)):
                m.plan[rows, cols] = (
                    scale * m.cs[yh, g : g + 1, :] * jnp.exp2(m.lg[step % 2, part_rows, cols] * exp2_scale)
                )

    arrived(m.cpr, *along_h, m.cp_send, m.cp_recv)
    m.bz[ITERS - 1, z] = total(m.cpr, nyh)
    start(m.bz.at[ITERS - 1], *along_z, m.z_send, m.z_recv.at[ITERS])
    for step in range(1, nyh):
        fill(step)
    finish(m.rsum, *along_h, m.q_send, m.q_recv)
    for block in range(nyh):
        place = slice(block * per_block, (block + 1) * per_block)
        m.row_mass[place, :] = m.rsum[block, :per_block, :]
        m.row_weight[place, :] = m.rsum[block, per_block:, :] * cot_scale
    for move in moves:
        move.wait()
    finish(m.bz0, *along_z, m.z0_send, m.z_recv.at[0])
    col_sums = total(m.bz0, nz)
    col_mass, col_weight = col_sums[0], col_sums[1] * cot_scale
    finish(m.bz.at[ITERS - 1], *along_z, m.z_send, m.z_recv.at[ITERS])
    col_dual = (col_weight - total(m.bz.at[ITERS - 1], nz)) / col_mass

    def column_part(row_dual, k):
        found = [jnp.zeros((8, LANES), F32)] * groups
        for i in range(chunks):
            dual = down(row_dual[i : i + 1, :])
            for g, cols in enumerate(tiles_of(groups)):
                found[g] = found[g] + fold(m.plan[i * LANES : (i + 1) * LANES, cols] * dual)
        for g in range(groups):
            m.bz[k, z, g : g + 1, :] = found[g].sum(0, keepdims=True)

    def row_part(col_dual, k):
        for i in range(chunks):
            rows = slice(i * LANES, (i + 1) * LANES)
            block = m.plan[rows, :LANES] * col_dual[0:1, :]
            for g, cols in enumerate(tiles_of(groups - 1, 1), 1):
                block = block + m.plan[rows, cols] * col_dual[g : g + 1, :]
            m.bx[k, xc, i : i + 1, :] = across(block)

    def sweep(k, duals):
        row_part(duals[1], k)
        start(m.bx.at[k], *along_x, m.x_send, m.x_recv.at[k])

        @pl.when(k == 0)
        def _():
            @pl.loop(0, chunks)
            def _(i):
                rows = aligned(i)
                m.splan[rows, :] = (m.plan[rows, :] * cot_scale).astype(BF16)

        finish(m.bx.at[k], *along_x, m.x_send, m.x_recv.at[k])
        m.by[k, y] = total(m.bx.at[k], nxc)
        start(m.by.at[k], *along_y, m.y_send, m.y_recv.at[k])

        @pl.when(k == 0)
        def _():
            @pl.loop(0, groups)
            def _(g):
                cols = aligned(g)
                m.tail[cols, :] = dot_tn(m.splan[:, cols], m.ev[1].reshape(chunks * LANES, width))

        finish(m.by.at[k], *along_y, m.y_send, m.y_recv.at[k])
        row_dual = (m.row_weight[...] - total(m.by.at[k], ny)) / m.row_mass[...]
        column_part(row_dual, k)
        start(m.bz.at[k], *along_z, m.z_send, m.z_recv.at[k + 1])
        finish(m.bz.at[k], *along_z, m.z_send, m.z_recv.at[k + 1])
        return row_dual, (col_weight - total(m.bz.at[k], nz)) / col_mass

    row_dual, col_dual = lax.fori_loop(
        0, ITERS - 1, sweep, (jnp.zeros((chunks, LANES), F32), col_dual)
    )

    m.bx[0, xc] = row_dual * (1.0 / cot_scale)
    col_scaled = col_dual * (1.0 / cot_scale)
    half = nx // per_block

    def last_chunk(block, h):
        i = block * per_block + h
        rows = aligned(i)
        dual = down(m.bx[0, xc, pl.ds(i, 1), :])
        for g, cols in enumerate(tiles_of(groups)):
            piece = m.plan[rows, cols] * (m.dot[rows, cols] - dual - col_scaled[g : g + 1, :])
            m.grad[rows, cols] = (cot_scale * logit_scale * piece).astype(BF16)
        product = jnp.dot(m.grad[rows, :], m.pr[yh], preferred_element_type=F32)
        m.eb[block, pl.ds(h * half, half)] = product.reshape(
            half, nyl, nc, LANES // (half * nyl * nc), width
        ).astype(BF16)

    for step in range(1, nyh + 1):
        block = (yh + step) % nyh

        for h in range(per_block):
            last_chunk(block, h)

        for turn in range(1, nxc):
            other = (xc + turn) % nxc
            sends.append(
                pltpu.make_async_remote_copy(
                    m.eb.at[block, other // nc, :, other % nc],
                    m.fx.at[block, xc],
                    m.fx_send.at[step - 1, turn],
                    m.fx_recv.at[block, xc],
                    at_xc(other),
                    MESH,
                )
            )
            sends[-1].start()
        if step < nyh:
            m.tail[...] += dot_tn(m.grad[aligned(block, per_block * LANES), :], block_rows(0, block))

    for step in far_first(nz) + [nz]:
        other = (z + step) % nz
        cols = aligned(other)
        share = m.tail[cols, :] + dot_tn(m.grad[own_rows, cols], block_rows(0, yh))
        if step < nz:
            m.pb[step] = share.astype(BF16)
            sends.append(
                pltpu.make_async_remote_copy(
                    m.pb.at[step], m.fz.at[z], m.fz_send.at[step], m.fz_recv.at[z], at_z(other), MESH
                )
            )
            sends[-1].start()
        else:
            pg_ref[...] = share

    for step in range(1, nyh + 1):
        block = (yh + step) % nyh
        arrived(m.fx.at[block], *along_x, m.fx_send.at[step - 1], m.fx_recv.at[block])
        part = m.eb[block, x, :, core].astype(F32)
        for turn in range(1, nxc):
            part = part + m.fx[block, (xc + turn) % nxc].astype(F32)
        m.fy_out[pl.ds(block * nyl, nyl)] = part
        for low in range(nyl):
            if step < nyh:
                other, slot = block * nyl + low, (step - 1) * nyl + low
            elif low:
                other, slot = yh * nyl + (yl + low) % nyl, (step - 1) * nyl + low
            else:
                continue
            sends.append(
                pltpu.make_async_remote_copy(
                    m.fy_out.at[other], m.fy.at[y], m.fy_send.at[slot], m.fy_recv.at[y], at_y(other), MESH
                )
            )
            sends[-1].start()

    arrived(m.fz, *along_z, m.fz_send, m.fz_recv)
    share = pg_ref[...]
    for step in range(1, nz):
        share = share + m.fz[(z + step) % nz].astype(F32)
    pg_ref[...] = share

    arrived(m.fy, *along_y, m.fy_send, m.fy_recv)
    rows_out = m.fy_out[y]
    for step in range(1, ny):
        rows_out = rows_out + m.fy[(y + step) % ny]
    eg_ref[...] = rows_out

    for send in sends:
        send.wait_send()


def build(mesh, dims):
    nx, nyl, nc, nyh, nz = dims
    ny, nxc, npr = nyl * nyh, nx * nc, nx * nyl * nc

    def per_device(embeddings, second_view, prototypes, row_scale, col_scale):
        row_count, width = embeddings.shape
        proto_count = prototypes.shape[0]
        proto_total = proto_count * npr
        rows, cols = row_count * nyh, proto_count // nyh
        per_block = row_count // LANES
        chunks, groups = rows // LANES, cols // LANES
        rows_out, cols_out = row_count // npr, cols // nz
        vmem, dma = pltpu.VMEM, pltpu.SemaphoreType.DMA
        scratch = dict(
            ev=vmem((2, chunks, LANES, width), BF16),
            pr=vmem((nyh, cols, width), BF16),
            rs=vmem((chunks, 1, LANES), F32),
            cs=vmem((nyh, groups, LANES), F32),
            plan0=vmem((nyh, row_count, cols), F32),
            dot0=vmem((nyh, row_count, cols), F32),
            plan=vmem((rows, cols), F32),
            dot=vmem((rows, cols), F32),
            lg=vmem((2, row_count, cols), F32),
            grad=vmem((rows, cols), BF16),
            splan=vmem((rows, cols), BF16),
            tail=vmem((cols, width), F32),
            rowm=vmem((per_block, LANES, LANES), F32),
            roww=vmem((per_block, LANES, LANES), F32),
            bw=vmem((npr, 2 * per_block, LANES), F32),
            rsum=vmem((nyh, 2 * per_block, LANES), F32),
            dual0=vmem((per_block, LANES), F32),
            row_mass=vmem((chunks, LANES), F32),
            row_weight=vmem((chunks, LANES), F32),
            cms=vmem((nyh, 2, groups, LANES), F32),
            cmr=vmem((nyh, 2, groups, LANES), F32),
            cps=vmem((nyh, groups, LANES), F32),
            cpr=vmem((nyh, groups, LANES), F32),
            bz0=vmem((nz, 2, groups, LANES), F32),
            bx=vmem((ITERS - 1, nxc, chunks, LANES), F32),
            by=vmem((ITERS - 1, ny, chunks, LANES), F32),
            bz=vmem((ITERS, nz, groups, LANES), F32),
            eb=vmem((nyh, nx, nyl, nc, rows_out, width), BF16),
            fx=vmem((nyh, nxc, nyl, rows_out, width), BF16),
            fy_out=vmem((ny, rows_out, width), F32),
            fy=vmem((ny, rows_out, width), F32),
            pb=vmem((nz, cols_out, width), BF16),
            fz=vmem((nz, cols_out, width), BF16),
            local_sem=dma((4,)),
            pro_sem=dma((nyh,)),
            g_send=dma((nyh,)),
            g_recv=dma((nyh,)),
            r_send=dma((nyh,)),
            r_recv=dma((nyh,)),
            c_send=dma((nyh,)),
            c_recv=dma((nyh,)),
            w_send=dma((npr,)),
            w_recv=dma((npr,)),
            q_send=dma((nyh,)),
            q_recv=dma((nyh,)),
            cm_send=dma((nyh,)),
            cm_recv=dma((nyh,)),
            cp_send=dma((nyh,)),
            cp_recv=dma((nyh,)),
            x_send=dma((nxc,)),
            y_send=dma((ny,)),
            z_send=dma((nz,)),
            z0_send=dma((nz,)),
            x_recv=dma((ITERS - 1, nxc)),
            y_recv=dma((ITERS - 1, ny)),
            z_recv=dma((ITERS + 1, nz)),
            fx_send=dma((nyh, nxc)),
            fx_recv=dma((nyh, nxc)),
            fy_send=dma((ny,)),
            fy_recv=dma((ny,)),
            fz_send=dma((nz,)),
            fz_recv=dma((nz,)),
        )
        return pl.pallas_call(
            functools.partial(kernel, dims, proto_total, tuple(scratch)),
            out_shape=(
                jax.ShapeDtypeStruct((rows_out, width), F32),
                jax.ShapeDtypeStruct((cols_out, width), F32),
            ),
            in_specs=[pl.BlockSpec(memory_space=pltpu.HBM)] * 5,
            out_specs=(pl.BlockSpec(memory_space=pltpu.VMEM),) * 2,
            scratch_shapes=list(scratch.values()),
            compiler_params=pltpu.CompilerParams(
                collective_id=0, has_side_effects=True, vmem_limit_bytes=40 * 1024 * 1024
            ),
        )(
            *[
                pltpu.with_memory_space_constraint(array, pltpu.HBM)
                for array in (
                    embeddings.reshape(per_block, LANES, width),
                    second_view.reshape(per_block, LANES, width),
                    prototypes.reshape(nyh, cols, width),
                    row_scale.reshape(per_block, 1, LANES),
                    col_scale.reshape(nyh, groups, LANES),
                )
            ]
        )

    return jax.shard_map(
        per_device,
        mesh=mesh,
        in_specs=(P("row", None), P("row", None), P("proto", None), P("row"), P("proto")),
        out_specs=(P(("row", "proto"), None), P(("proto", "row"), None)),
        check_vma=False,
    )


def solution(mesh):
    return build(mesh, DIMS)
```

```python
import functools
import math
from types import SimpleNamespace

import jax
import jax.numpy as jnp
from jax import lax
from jax.experimental import pallas as pl
from jax.experimental.pallas import tpu as pltpu
from jax.sharding import PartitionSpec as P

ITERS = 4
LANES = 128
MESH = pl.DeviceIdType.MESH
F32 = jnp.float32
BF16 = jnp.bfloat16

DIMS = (4, 2, 2, 4, 8)


def dot_nt(left, right):
    return lax.dot_general(left, right, (((1,), (1,)), ((), ())), preferred_element_type=F32)


def dot_tn(left, right):
    return lax.dot_general(left, right, (((0,), (0,)), ((), ())), preferred_element_type=F32)


def down(row):
    return jnp.broadcast_to(row, (LANES, LANES)).T


def fold(block):
    return block.reshape(block.shape[0] // 8, 8, LANES).sum(0)


def across(block):
    return block.T.sum(0, keepdims=True)


def tiles_of(count, start=0):
    return [slice((start + g) * LANES, (start + g + 1) * LANES) for g in range(count)]


def aligned(i, size=LANES):
    return pl.ds(pl.multiple_of(i * size, size), size)


def div(a, b):
    return lax.div(a, jnp.int32(b))


def rem(a, b):
    return lax.rem(a, jnp.int32(b))


def far_first(count):
    return sorted(range(1, count), key=lambda step: -min(step, count - step))


def kernel(dims, proto_total, names, emb_in, view_in, pro_in, rs_in, cs_in, eg_ref, pg_ref, *scratch):
    m = SimpleNamespace(**dict(zip(names, scratch)))
    nx, nyl, nc, nyh, nz = dims
    ny, nxc, npr = nyl * nyh, nx * nc, nx * nyl * nc
    row_id, me_p = lax.axis_index("row"), lax.axis_index("proto")
    yh, z = div(row_id, nz), rem(row_id, nz)
    core = rem(me_p, nc)
    yl = rem(div(me_p, nc), nyl)
    x = div(me_p, nc * nyl)
    y = yh * nyl + yl
    xc = x * nc + core

    def at_z(other):
        return (yh * nz + other, me_p)

    def at_yh(other):
        return (other * nz + z, me_p)

    def at_y(other):
        return (div(other, nyl) * nz + z, (x * nyl + rem(other, nyl)) * nc + core)

    def at_xc(other):
        return (row_id, (div(other, nc) * nyl + yl) * nc + rem(other, nc))

    def at_p(other):
        return (row_id, other)

    chunks, groups = m.plan.shape[0] // LANES, m.plan.shape[1] // LANES
    per_block = chunks // nyh
    width = emb_in.shape[-1]
    logit_scale = 1.0 / (0.05 * width)
    view_scale = 1.0 / (0.1 * width)
    mass_inverse = 1.0 / (64.0 * proto_total)
    view_shift = 2.0 ** math.ceil(-math.log2(view_scale))
    cot_scale = -view_scale * view_shift
    exp2_scale = logit_scale * math.log2(math.e)

    own = pl.ds(yh * per_block, per_block)
    small_loads = [
        pltpu.make_async_copy(emb_in, m.ev.at[0, own], m.local_sem.at[0]),
        pltpu.make_async_copy(view_in, m.ev.at[1, own], m.local_sem.at[1]),
        pltpu.make_async_copy(rs_in, m.rs.at[own], m.local_sem.at[2]),
        pltpu.make_async_copy(cs_in, m.cs, m.local_sem.at[3]),
    ]
    for load in small_loads:
        load.start()

    def pro_load(part):
        return pltpu.make_async_copy(pro_in.at[part], m.pr.at[part], m.pro_sem.at[part])

    for part in range(nyh):
        pro_load(part).start()

    barrier = pltpu.get_barrier_semaphore()
    for count, me, address in ((ny, y, at_y), (nz, z, at_z), (npr, me_p, at_p)):
        for step in far_first(count):
            pl.semaphore_signal(
                barrier, inc=1, device_id=address(rem(me + step, count)), device_id_type=MESH
            )
    for load in small_loads:
        load.wait()
    m.ev[1, own] = (m.ev[1, own].astype(F32) * (1.0 / view_shift)).astype(BF16)

    m.rowm[...] = jnp.zeros_like(m.rowm)
    m.roww[...] = jnp.zeros_like(m.roww)

    def own_part(part):
        for h in range(per_block):
            rows = slice(h * LANES, (h + 1) * LANES)
            scale = down(m.rs[yh * per_block + h]) * mass_inverse
            mass = m.rowm[h]
            weight = m.roww[h]
            for g, cols in enumerate(tiles_of(groups)):
                value = scale * m.cs[part, g : g + 1, :] * jnp.exp2(m.lg[part % 2, rows, cols] * exp2_scale)
                m.plan0[part, rows, cols] = value
                weighted = value * m.dot0[part, rows, cols]
                mass = mass + value
                weight = weight + weighted
            m.rowm[h] = mass
            m.roww[h] = weight

    def block_rows(kind, block):
        place = pl.ds(block * per_block, per_block)
        return m.ev[kind, place].reshape(per_block * LANES, width)

    def own_parts(first, last):
        for part in range(first, last):
            pro_load(part).wait()
        for part in range(first, last):
            m.lg[part % 2] = dot_nt(block_rows(0, yh), m.pr[part])
            m.dot0[part] = dot_nt(block_rows(1, yh), m.pr[part])
            own_part(part)

    own_parts(0, nyh // 2)
    own_parts(nyh // 2, nyh)
    sends = []

    def start(slots, me, count, address, send, recv):
        for step in far_first(count):
            other = rem(me + step, count)
            pltpu.make_async_remote_copy(
                slots.at[me], slots.at[me], send.at[step], recv.at[me], address(other), MESH
            ).start()

    def finish(slots, me, count, address, send, recv):
        for step in range(1, count):
            other = rem(me + step, count)
            pltpu.make_async_remote_copy(
                slots.at[other], slots.at[other], send.at[step], recv.at[other], address(other), MESH
            ).wait_recv()
        for step in range(1, count):
            other = rem(me + step, count)
            pltpu.make_async_remote_copy(
                slots.at[me], slots.at[me], send.at[step], recv.at[me], address(other), MESH
            ).wait_send()

    def scatter(shares, slots, me, count, address, send, recv):
        copies = []
        for step in far_first(count):
            other = rem(me + step, count)
            copies.append(
                pltpu.make_async_remote_copy(
                    shares.at[other], slots.at[me], send.at[step], recv.at[me], address(other), MESH
                )
            )
            copies[-1].start()
        return copies

    def arrived(slots, me, count, address, send, recv):
        for step in range(1, count):
            other = rem(me + step, count)
            pltpu.make_async_remote_copy(
                slots.at[other], slots.at[other], send.at[step], recv.at[other], address(other), MESH
            ).wait_recv()

    def total(slots, count):
        result = slots[0]
        for slot in range(1, count):
            result = result + slots[slot]
        return result

    along_x = (xc, nxc, at_xc)
    along_y = (y, ny, at_y)
    along_z = (z, nz, at_z)
    along_p = (me_p, npr, at_p)
    along_h = (yh, nyh, at_yh)

    for h in range(per_block):
        m.bw[me_p, h : h + 1, :] = across(m.rowm[h])
        m.bw[me_p, per_block + h : per_block + h + 1, :] = across(m.roww[h])
    pl.semaphore_wait(barrier, nz + ny + npr - 3)
    start(m.bw, *along_p, m.w_send, m.w_recv)

    sign = 2 * yl - 1
    partner = at_xc(x * nc + rem(core + 1, nc))
    blocks = []
    for step in range(1, nyh):
        target = rem(y + sign * step + ny, ny)
        source = rem(y + (sign if step % 2 else -sign) * step + ny, ny)
        origin = div(source, nyl)
        blocks.append((origin, pl.ds(origin * per_block, per_block)))
        rows_out = pltpu.make_async_remote_copy(
            m.ev.at[core, own], m.ev.at[core, own], m.g_send.at[step], m.g_recv.at[step], at_y(target), MESH
        )
        scale_out = pltpu.make_async_remote_copy(
            m.rs.at[own], m.rs.at[own], m.r_send.at[step], m.r_recv.at[step], at_y(target), MESH
        )
        rows_out.start()
        scale_out.start()
        sends += [rows_out, scale_out]

    own_rows = aligned(yh, per_block * LANES)
    moves = [
        pltpu.make_async_copy(m.plan0.at[yh], m.plan.at[own_rows], m.local_sem.at[0]),
        pltpu.make_async_copy(m.dot0.at[yh], m.dot.at[own_rows], m.local_sem.at[1]),
    ]
    for move in moves:
        move.start()

    @pl.loop(0, nyh)
    def _(part):
        for g, cols in enumerate(tiles_of(groups)):
            value = m.plan0[part, :, cols]
            m.cms[part, 0, g : g + 1, :] = fold(value).sum(0, keepdims=True)
            value = value * m.dot0[part, :, cols]
            m.cms[part, 1, g : g + 1, :] = fold(value).sum(0, keepdims=True)

    sends += scatter(m.cms, m.cmr, *along_h, m.cm_send, m.cm_recv)
    m.cmr[yh] = m.cms[yh]

    finish(m.bw, *along_p, m.w_send, m.w_recv)
    sums = total(m.bw, npr)
    m.rsum[yh] = sums
    m.dual0[...] = sums[per_block:] * cot_scale / sums[:per_block]
    start(m.rsum, *along_h, m.q_send, m.q_recv)

    for part in range(nyh):
        found = [jnp.zeros((8, LANES), F32)] * groups
        for h in range(per_block):
            dual = down(m.dual0[h : h + 1, :])
            for g, cols in enumerate(tiles_of(groups)):
                found[g] = found[g] + fold(m.plan0[part, h * LANES : (h + 1) * LANES, cols] * dual)
        for g in range(groups):
            m.cps[part, g : g + 1, :] = found[g].sum(0, keepdims=True)

    sends += scatter(m.cps, m.cpr, *along_h, m.cp_send, m.cp_recv)
    m.cpr[yh] = m.cps[yh]

    for step, (block, there) in enumerate(blocks, 1):
        mine = m.ev.at[core, there]
        pltpu.make_async_remote_copy(
            mine, mine, m.g_send.at[step], m.g_recv.at[step], partner, MESH
        ).wait_recv()
        hand = pltpu.make_async_remote_copy(
            mine, mine, m.c_send.at[step], m.c_recv.at[step], partner, MESH
        )
        hand.start()
        sends.append(hand)

    arrived(m.cmr, *along_h, m.cm_send, m.cm_recv)
    m.bz0[z] = total(m.cmr, nyh)
    start(m.bz0, *along_z, m.z0_send, m.z_recv.at[0])

    def fill(step):
        block, there = blocks[step - 1]
        taken = m.ev.at[rem(core + 1, nc), there]
        scales = m.rs.at[there]
        pltpu.make_async_remote_copy(
            scales, scales, m.r_send.at[step], m.r_recv.at[step], partner, MESH
        ).wait_recv()
        pltpu.make_async_remote_copy(
            taken, taken, m.c_send.at[step], m.c_recv.at[step], partner, MESH
        ).wait_recv()

        m.lg[step % 2] = dot_nt(block_rows(0, block), m.pr[yh])
        m.dot[aligned(block, per_block * LANES), :] = dot_nt(block_rows(1, block), m.pr[yh])
        for h in range(per_block):
            i = block * per_block + h
            rows = aligned(i)
            part_rows = slice(h * LANES, (h + 1) * LANES)
            scale = down(m.rs[i]) * mass_inverse
            for g, cols in enumerate(tiles_of(groups)):
                m.plan[rows, cols] = (
                    scale * m.cs[yh, g : g + 1, :] * jnp.exp2(m.lg[step % 2, part_rows, cols] * exp2_scale)
                )

    arrived(m.cpr, *along_h, m.cp_send, m.cp_recv)
    m.bz[ITERS - 1, z] = total(m.cpr, nyh)
    start(m.bz.at[ITERS - 1], *along_z, m.z_send, m.z_recv.at[ITERS])
    for step in range(1, nyh):
        fill(step)
    finish(m.rsum, *along_h, m.q_send, m.q_recv)
    for block in range(nyh):
        place = slice(block * per_block, (block + 1) * per_block)
        m.row_mass[place, :] = m.rsum[block, :per_block, :]
        m.row_weight[place, :] = m.rsum[block, per_block:, :] * cot_scale
    for move in moves:
        move.wait()
    finish(m.bz0, *along_z, m.z0_send, m.z_recv.at[0])
    col_sums = total(m.bz0, nz)
    col_mass, col_weight = col_sums[0], col_sums[1] * cot_scale
    finish(m.bz.at[ITERS - 1], *along_z, m.z_send, m.z_recv.at[ITERS])
    col_dual = (col_weight - total(m.bz.at[ITERS - 1], nz)) / col_mass

    def column_part(row_dual, k):
        found = [jnp.zeros((8, LANES), F32)] * groups
        for i in range(chunks):
            dual = down(row_dual[i : i + 1, :])
            for g, cols in enumerate(tiles_of(groups)):
                found[g] = found[g] + fold(m.plan[i * LANES : (i + 1) * LANES, cols] * dual)
        for g in range(groups):
            m.bz[k, z, g : g + 1, :] = found[g].sum(0, keepdims=True)

    def row_part(col_dual, k):
        for i in range(chunks):
            rows = slice(i * LANES, (i + 1) * LANES)
            block = m.plan[rows, :LANES] * col_dual[0:1, :]
            for g, cols in enumerate(tiles_of(groups - 1, 1), 1):
                block = block + m.plan[rows, cols] * col_dual[g : g + 1, :]
            m.bx[k, xc, i : i + 1, :] = across(block)

    def sweep(k, col_dual):
        row_part(col_dual, k)
        start(m.bx.at[k], *along_x, m.x_send, m.x_recv.at[k])

        @pl.when(k == 0)
        def _():
            @pl.loop(0, chunks)
            def _(i):
                rows = aligned(i)
                m.splan[rows, :] = (m.plan[rows, :] * cot_scale).astype(BF16)

        finish(m.bx.at[k], *along_x, m.x_send, m.x_recv.at[k])
        m.by[k, y] = total(m.bx.at[k], nxc)
        start(m.by.at[k], *along_y, m.y_send, m.y_recv.at[k])

        @pl.when(k == 0)
        def _():
            @pl.loop(0, groups)
            def _(g):
                cols = aligned(g)
                m.tail[cols, :] = dot_tn(m.splan[:, cols], m.ev[1].reshape(chunks * LANES, width))

        finish(m.by.at[k], *along_y, m.y_send, m.y_recv.at[k])
        row_dual = (m.row_weight[...] - total(m.by.at[k], ny)) / m.row_mass[...]
        column_part(row_dual, k)
        start(m.bz.at[k], *along_z, m.z_send, m.z_recv.at[k + 1])

        @pl.when(k == ITERS - 2)
        def _():
            m.dual[...] = row_dual * (1.0 / cot_scale)

            @pl.loop(0, chunks)
            def _(i):
                rows = aligned(i)
                dual = down(m.dual[pl.ds(i, 1), :])
                for cols in tiles_of(groups):
                    piece = m.plan[rows, cols] * (m.dot[rows, cols] - dual)
                    m.dot[rows, cols] = piece * (cot_scale * logit_scale)

        finish(m.bz.at[k], *along_z, m.z_send, m.z_recv.at[k + 1])
        return (col_weight - total(m.bz.at[k], nz)) / col_mass

    col_dual = lax.fori_loop(0, ITERS - 1, sweep, col_dual)

    col_scaled = col_dual * logit_scale
    span = nyh // 2
    part_rows = span * per_block * LANES
    for turn_half in range(2):
        part = rem(div(yh, span) + 1 + turn_half, 2)

        @pl.loop(0, span * per_block)
        def _(i):
            rows = aligned(part * (span * per_block) + i)
            for g, cols in enumerate(tiles_of(groups)):
                piece = m.dot[rows, cols] - m.plan[rows, cols] * col_scaled[g : g + 1, :]
                m.grad[rows, cols] = piece.astype(BF16)

        product = jnp.dot(m.grad[aligned(part, part_rows), :], m.pr[yh], preferred_element_type=F32)
        m.eb[pl.ds(part * span, span)] = product.reshape(
            span, nx, nyl, nc, m.eb.shape[4], width
        ).astype(BF16)
        for low in range(span):
            block = part * span + low
            for turn in far_first(nxc):
                other = rem(xc + turn, nxc)
                sends.append(
                    pltpu.make_async_remote_copy(
                        m.eb.at[block, div(other, nc), :, rem(other, nc)],
                        m.fx.at[block, xc],
                        m.fx_send.at[turn_half * span + low, turn],
                        m.fx_recv.at[block, xc],
                        at_xc(other),
                        MESH,
                    )
                )
                sends[-1].start()

    share = m.tail[...] + dot_tn(m.grad[...], m.ev[0].reshape(chunks * LANES, width))
    m.tail[...] = share
    m.pb[...] = share.reshape(m.pb.shape).astype(BF16)
    for step in far_first(nz):
        other = rem(z + step, nz)
        sends.append(
            pltpu.make_async_remote_copy(
                m.pb.at[other], m.fz.at[z], m.fz_send.at[step], m.fz_recv.at[z], at_z(other), MESH
            )
        )
        sends[-1].start()

    for step in range(1, nyh + 1):
        block = rem(yh + step, nyh)
        arrived(m.fx.at[block], *along_x, m.fx_send.at[step - 1], m.fx_recv.at[block])
        part = m.eb[block, x, :, core].astype(F32)
        for turn in range(1, nxc):
            part = part + m.fx[block, rem(xc + turn, nxc)].astype(F32)
        m.fy_out[pl.ds(block * nyl, nyl)] = part
        for low in range(nyl):
            if step < nyh:
                other, slot = block * nyl + low, (step - 1) * nyl + low
            elif low:
                other, slot = yh * nyl + rem(yl + low, nyl), (step - 1) * nyl + low
            else:
                continue
            sends.append(
                pltpu.make_async_remote_copy(
                    m.fy_out.at[other], m.fy.at[y], m.fy_send.at[slot], m.fy_recv.at[y], at_y(other), MESH
                )
            )
            sends[-1].start()

    arrived(m.fz, *along_z, m.fz_send, m.fz_recv)
    share = m.tail[aligned(z, m.fz.shape[1]), :]
    for step in range(1, nz):
        share = share + m.fz[rem(z + step, nz)].astype(F32)
    pg_ref[...] = share

    arrived(m.fy, *along_y, m.fy_send, m.fy_recv)
    rows_out = m.fy_out[y]
    for step in range(1, ny):
        rows_out = rows_out + m.fy[rem(y + step, ny)]
    eg_ref[...] = rows_out

    for send in sends:
        send.wait_send()


def build(mesh, dims):
    nx, nyl, nc, nyh, nz = dims
    ny, nxc, npr = nyl * nyh, nx * nc, nx * nyl * nc

    def per_device(embeddings, second_view, prototypes, row_scale, col_scale):
        row_count, width = embeddings.shape
        proto_count = prototypes.shape[0]
        proto_total = proto_count * npr
        rows, cols = row_count * nyh, proto_count // nyh
        per_block = row_count // LANES
        chunks, groups = rows // LANES, cols // LANES
        rows_out, cols_out = row_count // npr, cols // nz
        vmem, dma = pltpu.VMEM, pltpu.SemaphoreType.DMA
        scratch = dict(
            ev=vmem((2, chunks, LANES, width), BF16),
            pr=vmem((nyh, cols, width), BF16),
            rs=vmem((chunks, 1, LANES), F32),
            cs=vmem((nyh, groups, LANES), F32),
            plan0=vmem((nyh, row_count, cols), F32),
            dot0=vmem((nyh, row_count, cols), F32),
            plan=vmem((rows, cols), F32),
            dot=vmem((rows, cols), F32),
            lg=vmem((2, row_count, cols), F32),
            grad=vmem((rows, cols), BF16),
            splan=vmem((rows, cols), BF16),
            tail=vmem((cols, width), F32),
            rowm=vmem((per_block, LANES, LANES), F32),
            roww=vmem((per_block, LANES, LANES), F32),
            bw=vmem((npr, 2 * per_block, LANES), F32),
            rsum=vmem((nyh, 2 * per_block, LANES), F32),
            dual0=vmem((per_block, LANES), F32),
            dual=vmem((chunks, LANES), F32),
            row_mass=vmem((chunks, LANES), F32),
            row_weight=vmem((chunks, LANES), F32),
            cms=vmem((nyh, 2, groups, LANES), F32),
            cmr=vmem((nyh, 2, groups, LANES), F32),
            cps=vmem((nyh, groups, LANES), F32),
            cpr=vmem((nyh, groups, LANES), F32),
            bz0=vmem((nz, 2, groups, LANES), F32),
            bx=vmem((ITERS - 1, nxc, chunks, LANES), F32),
            by=vmem((ITERS - 1, ny, chunks, LANES), F32),
            bz=vmem((ITERS, nz, groups, LANES), F32),
            eb=vmem((nyh, nx, nyl, nc, rows_out, width), BF16),
            fx=vmem((nyh, nxc, nyl, rows_out, width), BF16),
            fy_out=vmem((ny, rows_out, width), F32),
            fy=vmem((ny, rows_out, width), F32),
            pb=vmem((nz, cols_out, width), BF16),
            fz=vmem((nz, cols_out, width), BF16),
            local_sem=dma((4,)),
            pro_sem=dma((nyh,)),
            g_send=dma((nyh,)),
            g_recv=dma((nyh,)),
            r_send=dma((nyh,)),
            r_recv=dma((nyh,)),
            c_send=dma((nyh,)),
            c_recv=dma((nyh,)),
            w_send=dma((npr,)),
            w_recv=dma((npr,)),
            q_send=dma((nyh,)),
            q_recv=dma((nyh,)),
            cm_send=dma((nyh,)),
            cm_recv=dma((nyh,)),
            cp_send=dma((nyh,)),
            cp_recv=dma((nyh,)),
            x_send=dma((nxc,)),
            y_send=dma((ny,)),
            z_send=dma((nz,)),
            z0_send=dma((nz,)),
            x_recv=dma((ITERS - 1, nxc)),
            y_recv=dma((ITERS - 1, ny)),
            z_recv=dma((ITERS + 1, nz)),
            fx_send=dma((nyh, nxc)),
            fx_recv=dma((nyh, nxc)),
            fy_send=dma((ny,)),
            fy_recv=dma((ny,)),
            fz_send=dma((nz,)),
            fz_recv=dma((nz,)),
        )
        return pl.pallas_call(
            functools.partial(kernel, dims, proto_total, tuple(scratch)),
            out_shape=(
                jax.ShapeDtypeStruct((rows_out, width), F32),
                jax.ShapeDtypeStruct((cols_out, width), F32),
            ),
            in_specs=[pl.BlockSpec(memory_space=pltpu.HBM)] * 5,
            out_specs=(pl.BlockSpec(memory_space=pltpu.VMEM),) * 2,
            scratch_shapes=list(scratch.values()),
            compiler_params=pltpu.CompilerParams(
                collective_id=0, has_side_effects=True, vmem_limit_bytes=40 * 1024 * 1024
            ),
        )(
            *[
                pltpu.with_memory_space_constraint(array, pltpu.HBM)
                for array in (
                    embeddings.reshape(per_block, LANES, width),
                    second_view.reshape(per_block, LANES, width),
                    prototypes.reshape(nyh, cols, width),
                    row_scale.reshape(per_block, 1, LANES),
                    col_scale.reshape(nyh, groups, LANES),
                )
            ]
        )

    return jax.shard_map(
        per_device,
        mesh=mesh,
        in_specs=(P("row", None), P("row", None), P("proto", None), P("row"), P("proto")),
        out_specs=(P(("row", "proto"), None), P(("proto", "row"), None)),
        check_vma=False,
    )


def solution(mesh):
    return build(mesh, DIMS)
```

```python
import functools
import math
from types import SimpleNamespace

import jax
import jax.numpy as jnp
from jax import lax
from jax.experimental import pallas as pl
from jax.experimental.pallas import tpu as pltpu
from jax.sharding import PartitionSpec as P

ITERS = 4
LANES = 128
MESH = pl.DeviceIdType.MESH
F32 = jnp.float32
BF16 = jnp.bfloat16

DIMS = (4, 2, 2, 4, 8)


def dot_nt(left, right):
    return lax.dot_general(left, right, (((1,), (1,)), ((), ())), preferred_element_type=F32)


def dot_tn(left, right):
    return lax.dot_general(left, right, (((0,), (0,)), ((), ())), preferred_element_type=F32)


def down(row):
    return jnp.broadcast_to(row, (LANES, LANES)).T


def fold(block):
    return block.reshape(block.shape[0] // 8, 8, LANES).sum(0)


def across(block):
    return block.T.sum(0, keepdims=True)


def tiles_of(count, start=0):
    return [slice((start + g) * LANES, (start + g + 1) * LANES) for g in range(count)]


def aligned(i, size=LANES):
    return pl.ds(pl.multiple_of(i * size, size), size)


def div(a, b):
    return lax.div(a, jnp.int32(b))


def rem(a, b):
    return lax.rem(a, jnp.int32(b))


def far_first(count):
    return sorted(range(1, count), key=lambda step: -min(step, count - step))


def kernel(dims, proto_total, names, emb_in, view_in, pro_in, rs_in, cs_in, eg_ref, pg_ref, *scratch):
    m = SimpleNamespace(**dict(zip(names, scratch)))
    nx, nyl, nc, nyh, nz = dims
    ny, nxc, npr = nyl * nyh, nx * nc, nx * nyl * nc
    row_id, me_p = lax.axis_index("row"), lax.axis_index("proto")
    yh, z = div(row_id, nz), rem(row_id, nz)
    core = rem(me_p, nc)
    yl = rem(div(me_p, nc), nyl)
    x = div(me_p, nc * nyl)
    y = yh * nyl + yl
    xc = x * nc + core

    def at_z(other):
        return (yh * nz + other, me_p)

    def at_yh(other):
        return (other * nz + z, me_p)

    def at_y(other):
        return (div(other, nyl) * nz + z, (x * nyl + rem(other, nyl)) * nc + core)

    def at_xc(other):
        return (row_id, (div(other, nc) * nyl + yl) * nc + rem(other, nc))

    def at_p(other):
        return (row_id, other)

    chunks, groups = m.plan.shape[0] // LANES, m.plan.shape[1] // LANES
    per_block = chunks // nyh
    width = emb_in.shape[-1]
    logit_scale = 1.0 / (0.05 * width)
    view_scale = 1.0 / (0.1 * width)
    mass_inverse = 1.0 / (64.0 * proto_total)
    view_shift = 2.0 ** math.ceil(-math.log2(view_scale))
    cot_scale = -view_scale * view_shift
    exp2_scale = logit_scale * math.log2(math.e)

    own = pl.ds(yh * per_block, per_block)
    small_loads = [
        pltpu.make_async_copy(emb_in, m.ev.at[0, own], m.local_sem.at[0]),
        pltpu.make_async_copy(view_in, m.ev.at[1, own], m.local_sem.at[1]),
        pltpu.make_async_copy(rs_in, m.rs.at[own], m.local_sem.at[2]),
        pltpu.make_async_copy(cs_in, m.cs, m.local_sem.at[3]),
    ]
    for load in small_loads:
        load.start()

    def pro_load(part):
        return pltpu.make_async_copy(pro_in.at[part], m.pr.at[part], m.pro_sem.at[part])

    for part in range(nyh):
        pro_load(part).start()

    barrier = pltpu.get_barrier_semaphore()
    for count, me, address in ((ny, y, at_y), (nz, z, at_z), (npr, me_p, at_p)):
        for step in far_first(count):
            pl.semaphore_signal(
                barrier, inc=1, device_id=address(rem(me + step, count)), device_id_type=MESH
            )
    for load in small_loads:
        load.wait()
    m.ev[1, own] = (m.ev[1, own].astype(F32) * (1.0 / view_shift)).astype(BF16)

    m.rowm[...] = jnp.zeros_like(m.rowm)
    m.roww[...] = jnp.zeros_like(m.roww)

    def own_part(part):
        for h in range(per_block):
            rows = slice(h * LANES, (h + 1) * LANES)
            scale = down(m.rs[yh * per_block + h]) * mass_inverse
            mass = m.rowm[h]
            weight = m.roww[h]
            for g, cols in enumerate(tiles_of(groups)):
                value = scale * m.cs[part, g : g + 1, :] * jnp.exp2(m.lg[part % 2, rows, cols] * exp2_scale)
                m.plan0[part, rows, cols] = value
                weighted = value * m.dot0[part, rows, cols]
                mass = mass + value
                weight = weight + weighted
            m.rowm[h] = mass
            m.roww[h] = weight

    def block_rows(kind, block):
        place = pl.ds(block * per_block, per_block)
        return m.ev[kind, place].reshape(per_block * LANES, width)

    def own_parts(first, last):
        for part in range(first, last):
            pro_load(part).wait()
        for part in range(first, last):
            m.lg[part % 2] = dot_nt(block_rows(0, yh), m.pr[part])
            m.dot0[part] = dot_nt(block_rows(1, yh), m.pr[part])
            own_part(part)

    for part in range(nyh):
        own_parts(part, part + 1)
    sends = []

    def start(slots, me, count, address, send, recv):
        for step in far_first(count):
            other = rem(me + step, count)
            pltpu.make_async_remote_copy(
                slots.at[me], slots.at[me], send.at[step], recv.at[me], address(other), MESH
            ).start()

    def finish(slots, me, count, address, send, recv):
        for step in range(1, count):
            other = rem(me + step, count)
            pltpu.make_async_remote_copy(
                slots.at[other], slots.at[other], send.at[step], recv.at[other], address(other), MESH
            ).wait_recv()
        for step in range(1, count):
            other = rem(me + step, count)
            pltpu.make_async_remote_copy(
                slots.at[me], slots.at[me], send.at[step], recv.at[me], address(other), MESH
            ).wait_send()

    def scatter(shares, slots, me, count, address, send, recv):
        copies = []
        for step in far_first(count):
            other = rem(me + step, count)
            copies.append(
                pltpu.make_async_remote_copy(
                    shares.at[other], slots.at[me], send.at[step], recv.at[me], address(other), MESH
                )
            )
            copies[-1].start()
        return copies

    def arrived(slots, me, count, address, send, recv):
        for step in range(1, count):
            other = rem(me + step, count)
            pltpu.make_async_remote_copy(
                slots.at[other], slots.at[other], send.at[step], recv.at[other], address(other), MESH
            ).wait_recv()

    def total(slots, count):
        result = slots[0]
        for slot in range(1, count):
            result = result + slots[slot]
        return result

    along_x = (xc, nxc, at_xc)
    along_y = (y, ny, at_y)
    along_z = (z, nz, at_z)
    along_p = (me_p, npr, at_p)
    along_h = (yh, nyh, at_yh)

    for h in range(per_block):
        m.bw[me_p, h : h + 1, :] = across(m.rowm[h])
        m.bw[me_p, per_block + h : per_block + h + 1, :] = across(m.roww[h])
    pl.semaphore_wait(barrier, nz + ny + npr - 3)
    start(m.bw, *along_p, m.w_send, m.w_recv)

    sign = 2 * yl - 1
    partner = at_xc(x * nc + rem(core + 1, nc))
    blocks = []
    for step in range(1, nyh):
        target = rem(y + sign * step + ny, ny)
        source = rem(y + (sign if step % 2 else -sign) * step + ny, ny)
        origin = div(source, nyl)
        blocks.append((origin, pl.ds(origin * per_block, per_block)))
        rows_out = pltpu.make_async_remote_copy(
            m.ev.at[core, own], m.ev.at[core, own], m.g_send.at[step], m.g_recv.at[step], at_y(target), MESH
        )
        scale_out = pltpu.make_async_remote_copy(
            m.rs.at[own], m.rs.at[own], m.r_send.at[step], m.r_recv.at[step], at_y(target), MESH
        )
        rows_out.start()
        scale_out.start()
        sends += [rows_out, scale_out]

    own_rows = aligned(yh, per_block * LANES)
    moves = [
        pltpu.make_async_copy(m.plan0.at[yh], m.plan.at[own_rows], m.local_sem.at[0]),
        pltpu.make_async_copy(m.dot0.at[yh], m.dot.at[own_rows], m.local_sem.at[1]),
    ]
    for move in moves:
        move.start()

    @pl.loop(0, nyh)
    def _(part):
        for g, cols in enumerate(tiles_of(groups)):
            value = m.plan0[part, :, cols]
            m.cms[part, 0, g : g + 1, :] = fold(value).sum(0, keepdims=True)
            value = value * m.dot0[part, :, cols]
            m.cms[part, 1, g : g + 1, :] = fold(value).sum(0, keepdims=True)

    sends += scatter(m.cms, m.cmr, *along_h, m.cm_send, m.cm_recv)
    m.cmr[yh] = m.cms[yh]

    finish(m.bw, *along_p, m.w_send, m.w_recv)
    sums = total(m.bw, npr)
    m.rsum[yh] = sums
    m.dual0[...] = sums[per_block:] * cot_scale / sums[:per_block]
    start(m.rsum, *along_h, m.q_send, m.q_recv)

    for part in range(nyh):
        found = [jnp.zeros((8, LANES), F32)] * groups
        for h in range(per_block):
            dual = down(m.dual0[h : h + 1, :])
            for g, cols in enumerate(tiles_of(groups)):
                found[g] = found[g] + fold(m.plan0[part, h * LANES : (h + 1) * LANES, cols] * dual)
        for g in range(groups):
            m.cps[part, g : g + 1, :] = found[g].sum(0, keepdims=True)

    sends += scatter(m.cps, m.cpr, *along_h, m.cp_send, m.cp_recv)
    m.cpr[yh] = m.cps[yh]

    for step, (block, there) in enumerate(blocks, 1):
        mine = m.ev.at[core, there]
        pltpu.make_async_remote_copy(
            mine, mine, m.g_send.at[step], m.g_recv.at[step], partner, MESH
        ).wait_recv()
        hand = pltpu.make_async_remote_copy(
            mine, mine, m.c_send.at[step], m.c_recv.at[step], partner, MESH
        )
        hand.start()
        sends.append(hand)

    arrived(m.cmr, *along_h, m.cm_send, m.cm_recv)
    m.bz0[z] = total(m.cmr, nyh)
    start(m.bz0, *along_z, m.z0_send, m.z_recv.at[0])

    def fill(step):
        block, there = blocks[step - 1]
        taken = m.ev.at[rem(core + 1, nc), there]
        scales = m.rs.at[there]
        pltpu.make_async_remote_copy(
            scales, scales, m.r_send.at[step], m.r_recv.at[step], partner, MESH
        ).wait_recv()
        pltpu.make_async_remote_copy(
            taken, taken, m.c_send.at[step], m.c_recv.at[step], partner, MESH
        ).wait_recv()

        m.lg[step % 2] = dot_nt(block_rows(0, block), m.pr[yh])
        m.dot[aligned(block, per_block * LANES), :] = dot_nt(block_rows(1, block), m.pr[yh])
        for h in range(per_block):
            i = block * per_block + h
            rows = aligned(i)
            part_rows = slice(h * LANES, (h + 1) * LANES)
            scale = down(m.rs[i]) * mass_inverse
            for g, cols in enumerate(tiles_of(groups)):
                m.plan[rows, cols] = (
                    scale * m.cs[yh, g : g + 1, :] * jnp.exp2(m.lg[step % 2, part_rows, cols] * exp2_scale)
                )

    arrived(m.cpr, *along_h, m.cp_send, m.cp_recv)
    m.bz[ITERS - 1, z] = total(m.cpr, nyh)
    start(m.bz.at[ITERS - 1], *along_z, m.z_send, m.z_recv.at[ITERS])
    for step in range(1, nyh):
        fill(step)
    finish(m.rsum, *along_h, m.q_send, m.q_recv)
    for block in range(nyh):
        place = slice(block * per_block, (block + 1) * per_block)
        m.row_mass[place, :] = m.rsum[block, :per_block, :]
        m.row_weight[place, :] = m.rsum[block, per_block:, :] * cot_scale
    for move in moves:
        move.wait()
    finish(m.bz0, *along_z, m.z0_send, m.z_recv.at[0])
    col_sums = total(m.bz0, nz)
    col_mass, col_weight = col_sums[0], col_sums[1] * cot_scale
    finish(m.bz.at[ITERS - 1], *along_z, m.z_send, m.z_recv.at[ITERS])
    col_dual = (col_weight - total(m.bz.at[ITERS - 1], nz)) / col_mass

    def column_part(row_dual, k):
        found = [jnp.zeros((8, LANES), F32)] * groups
        for i in range(chunks):
            dual = down(row_dual[i : i + 1, :])
            for g, cols in enumerate(tiles_of(groups)):
                found[g] = found[g] + fold(m.plan[i * LANES : (i + 1) * LANES, cols] * dual)
        for g in range(groups):
            m.bz[k, z, g : g + 1, :] = found[g].sum(0, keepdims=True)

    def row_part(col_dual, k):
        for i in range(chunks):
            rows = slice(i * LANES, (i + 1) * LANES)
            block = m.plan[rows, :LANES] * col_dual[0:1, :]
            for g, cols in enumerate(tiles_of(groups - 1, 1), 1):
                block = block + m.plan[rows, cols] * col_dual[g : g + 1, :]
            m.bx[k, xc, i : i + 1, :] = across(block)

    def sweep(k, col_dual):
        row_part(col_dual, k)
        start(m.bx.at[k], *along_x, m.x_send, m.x_recv.at[k])

        @pl.when(k == 0)
        def _():
            @pl.loop(0, chunks)
            def _(i):
                rows = aligned(i)
                m.splan[rows, :] = (m.plan[rows, :] * cot_scale).astype(BF16)

        finish(m.bx.at[k], *along_x, m.x_send, m.x_recv.at[k])
        m.by[k, y] = total(m.bx.at[k], nxc)
        start(m.by.at[k], *along_y, m.y_send, m.y_recv.at[k])

        @pl.when(k == 0)
        def _():
            @pl.loop(0, groups)
            def _(g):
                cols = aligned(g)
                m.tail[cols, :] = dot_tn(m.splan[:, cols], m.ev[1].reshape(chunks * LANES, width))

        finish(m.by.at[k], *along_y, m.y_send, m.y_recv.at[k])
        row_dual = (m.row_weight[...] - total(m.by.at[k], ny)) / m.row_mass[...]
        column_part(row_dual, k)
        start(m.bz.at[k], *along_z, m.z_send, m.z_recv.at[k + 1])

        @pl.when(k == ITERS - 2)
        def _():
            m.dual[...] = row_dual * (1.0 / cot_scale)

            @pl.loop(0, chunks)
            def _(i):
                rows = aligned(i)
                dual = down(m.dual[pl.ds(i, 1), :])
                for cols in tiles_of(groups):
                    piece = m.plan[rows, cols] * (m.dot[rows, cols] - dual)
                    m.dot[rows, cols] = piece * (cot_scale * logit_scale)

        finish(m.bz.at[k], *along_z, m.z_send, m.z_recv.at[k + 1])
        return (col_weight - total(m.bz.at[k], nz)) / col_mass

    col_dual = lax.fori_loop(0, ITERS - 1, sweep, col_dual)

    col_scaled = col_dual * logit_scale

    def last_block(block):
        for h in range(per_block):
            rows = aligned(block * per_block + h)
            for g, cols in enumerate(tiles_of(groups)):
                piece = m.dot[rows, cols] - m.plan[rows, cols] * col_scaled[g : g + 1, :]
                m.grad[rows, cols] = piece.astype(BF16)

    def send_block(step, block):
        rows = aligned(block, per_block * LANES)
        product = jnp.dot(m.grad[rows, :], m.pr[yh], preferred_element_type=F32)
        m.eb[block] = product.reshape(m.eb.shape[1:]).astype(BF16)
        for turn in range(1, nxc):
            other = rem(xc + turn, nxc)
            sends.append(
                pltpu.make_async_remote_copy(
                    m.eb.at[block, div(other, nc), :, rem(other, nc)],
                    m.fx.at[block, xc],
                    m.fx_send.at[step - 1, turn],
                    m.fx_recv.at[block, xc],
                    at_xc(other),
                    MESH,
                )
            )
            sends[-1].start()

    for step in range(1, nyh):
        block = rem(yh + step, nyh)
        last_block(block)
        send_block(step, block)

    last_block(yh)
    share = m.tail[...] + dot_tn(m.grad[...], m.ev[0].reshape(chunks * LANES, width))
    m.tail[...] = share
    m.pb[...] = share.reshape(m.pb.shape).astype(BF16)
    for step in far_first(nz):
        other = rem(z + step, nz)
        sends.append(
            pltpu.make_async_remote_copy(
                m.pb.at[other], m.fz.at[z], m.fz_send.at[step], m.fz_recv.at[z], at_z(other), MESH
            )
        )
        sends[-1].start()
    send_block(nyh, yh)

    for step in range(1, nyh + 1):
        block = rem(yh + step, nyh)
        arrived(m.fx.at[block], *along_x, m.fx_send.at[step - 1], m.fx_recv.at[block])
        part = m.eb[block, x, :, core].astype(F32)
        for turn in range(1, nxc):
            part = part + m.fx[block, rem(xc + turn, nxc)].astype(F32)
        m.fy_out[pl.ds(block * nyl, nyl)] = part
        for low in range(nyl):
            if step < nyh:
                other, slot = block * nyl + low, (step - 1) * nyl + low
            elif low:
                other, slot = yh * nyl + rem(yl + low, nyl), (step - 1) * nyl + low
            else:
                continue
            sends.append(
                pltpu.make_async_remote_copy(
                    m.fy_out.at[other], m.fy.at[y], m.fy_send.at[slot], m.fy_recv.at[y], at_y(other), MESH
                )
            )
            sends[-1].start()

    arrived(m.fz, *along_z, m.fz_send, m.fz_recv)
    share = m.tail[aligned(z, m.fz.shape[1]), :]
    for step in range(1, nz):
        share = share + m.fz[rem(z + step, nz)].astype(F32)
    pg_ref[...] = share

    arrived(m.fy, *along_y, m.fy_send, m.fy_recv)
    rows_out = m.fy_out[y]
    for step in range(1, ny):
        rows_out = rows_out + m.fy[rem(y + step, ny)]
    eg_ref[...] = rows_out

    for send in sends:
        send.wait_send()


def build(mesh, dims):
    nx, nyl, nc, nyh, nz = dims
    ny, nxc, npr = nyl * nyh, nx * nc, nx * nyl * nc

    def per_device(embeddings, second_view, prototypes, row_scale, col_scale):
        row_count, width = embeddings.shape
        proto_count = prototypes.shape[0]
        proto_total = proto_count * npr
        rows, cols = row_count * nyh, proto_count // nyh
        per_block = row_count // LANES
        chunks, groups = rows // LANES, cols // LANES
        rows_out, cols_out = row_count // npr, cols // nz
        vmem, dma = pltpu.VMEM, pltpu.SemaphoreType.DMA
        scratch = dict(
            ev=vmem((2, chunks, LANES, width), BF16),
            pr=vmem((nyh, cols, width), BF16),
            rs=vmem((chunks, 1, LANES), F32),
            cs=vmem((nyh, groups, LANES), F32),
            plan0=vmem((nyh, row_count, cols), F32),
            dot0=vmem((nyh, row_count, cols), F32),
            plan=vmem((rows, cols), F32),
            dot=vmem((rows, cols), F32),
            lg=vmem((2, row_count, cols), F32),
            grad=vmem((rows, cols), BF16),
            splan=vmem((rows, cols), BF16),
            tail=vmem((cols, width), F32),
            rowm=vmem((per_block, LANES, LANES), F32),
            roww=vmem((per_block, LANES, LANES), F32),
            bw=vmem((npr, 2 * per_block, LANES), F32),
            rsum=vmem((nyh, 2 * per_block, LANES), F32),
            dual0=vmem((per_block, LANES), F32),
            dual=vmem((chunks, LANES), F32),
            row_mass=vmem((chunks, LANES), F32),
            row_weight=vmem((chunks, LANES), F32),
            cms=vmem((nyh, 2, groups, LANES), F32),
            cmr=vmem((nyh, 2, groups, LANES), F32),
            cps=vmem((nyh, groups, LANES), F32),
            cpr=vmem((nyh, groups, LANES), F32),
            bz0=vmem((nz, 2, groups, LANES), F32),
            bx=vmem((ITERS - 1, nxc, chunks, LANES), F32),
            by=vmem((ITERS - 1, ny, chunks, LANES), F32),
            bz=vmem((ITERS, nz, groups, LANES), F32),
            eb=vmem((nyh, nx, nyl, nc, rows_out, width), BF16),
            fx=vmem((nyh, nxc, nyl, rows_out, width), BF16),
            fy_out=vmem((ny, rows_out, width), F32),
            fy=vmem((ny, rows_out, width), F32),
            pb=vmem((nz, cols_out, width), BF16),
            fz=vmem((nz, cols_out, width), BF16),
            local_sem=dma((4,)),
            pro_sem=dma((nyh,)),
            g_send=dma((nyh,)),
            g_recv=dma((nyh,)),
            r_send=dma((nyh,)),
            r_recv=dma((nyh,)),
            c_send=dma((nyh,)),
            c_recv=dma((nyh,)),
            w_send=dma((npr,)),
            w_recv=dma((npr,)),
            q_send=dma((nyh,)),
            q_recv=dma((nyh,)),
            cm_send=dma((nyh,)),
            cm_recv=dma((nyh,)),
            cp_send=dma((nyh,)),
            cp_recv=dma((nyh,)),
            x_send=dma((nxc,)),
            y_send=dma((ny,)),
            z_send=dma((nz,)),
            z0_send=dma((nz,)),
            x_recv=dma((ITERS - 1, nxc)),
            y_recv=dma((ITERS - 1, ny)),
            z_recv=dma((ITERS + 1, nz)),
            fx_send=dma((nyh, nxc)),
            fx_recv=dma((nyh, nxc)),
            fy_send=dma((ny,)),
            fy_recv=dma((ny,)),
            fz_send=dma((nz,)),
            fz_recv=dma((nz,)),
        )
        return pl.pallas_call(
            functools.partial(kernel, dims, proto_total, tuple(scratch)),
            out_shape=(
                jax.ShapeDtypeStruct((rows_out, width), F32),
                jax.ShapeDtypeStruct((cols_out, width), F32),
            ),
            in_specs=[pl.BlockSpec(memory_space=pltpu.HBM)] * 5,
            out_specs=(pl.BlockSpec(memory_space=pltpu.VMEM),) * 2,
            scratch_shapes=list(scratch.values()),
            compiler_params=pltpu.CompilerParams(
                collective_id=0, has_side_effects=True, vmem_limit_bytes=40 * 1024 * 1024
            ),
        )(
            *[
                pltpu.with_memory_space_constraint(array, pltpu.HBM)
                for array in (
                    embeddings.reshape(per_block, LANES, width),
                    second_view.reshape(per_block, LANES, width),
                    prototypes.reshape(nyh, cols, width),
                    row_scale.reshape(per_block, 1, LANES),
                    col_scale.reshape(nyh, groups, LANES),
                )
            ]
        )

    return jax.shard_map(
        per_device,
        mesh=mesh,
        in_specs=(P("row", None), P("row", None), P("proto", None), P("row"), P("proto")),
        out_specs=(P(("row", "proto"), None), P(("proto", "row"), None)),
        check_vma=False,
    )


def solution(mesh):
    return build(mesh, DIMS)
```
